128 devices in a mesh: dp: 32 (over x, z, y_lo), mp: 4 (over y_hi, core).
Axes of the slice: x: 4, y: 4 (y_hi: 2, y_lo: 2; y = y_hi * 2 + y_lo), z: 4, core: 2. Of those that a mesh axis runs over, the one named last changes fastest.
Arguments:
- inputs: bfloat16 [12288, 8192], P('dp', 'mp'), may hold values from -6 to 6
- gate_preact: bfloat16 [12288, 28672], P('dp', 'mp'), may hold values from -6 to 6
- hidden_grad: bfloat16 [12288, 28672], P('dp', 'mp'), may hold values from -0.109375 to 0.109375
- projector: bfloat16 [8192, 512], P('mp'), may hold values from -0.0625 to 0.0625
- first_moment: float32 [28672, 512], P(('mp', 'dp')), may hold values from -0.6 to 0.6
- second_moment: float32 [28672, 512], P(('mp', 'dp')), may hold values from 0.01 to 0.1
Outputs:
- new_first: float32 [28672, 512], P(('mp', 'dp'))
- new_second: float32 [28672, 512], P(('mp', 'dp'))
- weight_update: bfloat16 [28672, 8192], P(('mp', 'dp'))
The draws below stay inside these ranges and needn't reach their ends.
All inputs are finite; a program needn't handle non-finite values.
Results may differ from the reference program's by a relative error of at most 0.0058.
Values may be sent and summed in bfloat16 or wider, within the bound.
No kernel may reach another device: no remote copies, remote signals or barrier semaphores. Data moves between devices by JAX's collectives and lax.ppermute only.
A program may use at most 128 MiB of HBM per device.

```python
import math
import jax
import jax.numpy as jnp

D = 8192
FF = 28672
RANK = 512
TOKENS = 12288


def raised(drawn, stream_key, source, target, parts, factor):
    owner, partner = [(jnp.arange(drawn.shape[dim]) // (drawn.shape[dim] // parts)).reshape([-1 if axis == dim else 1 for axis in range(drawn.ndim)]) for dim in (source, target)]
    chosen = jax.random.permutation(stream_key, parts)[partner]
    strong = (owner == chosen) | (owner == (partner + parts // 2) % parts)
    return jnp.where(strong, factor * drawn, drawn)


def block_levels(rng, shape, cuts, smallest, largest):
    level, own = 1.0, jax.random.fold_in(rng, 6)
    for position, shards_of in cuts:
        heights = jnp.exp(jax.random.uniform(jax.random.fold_in(own, position), (shards_of,), jnp.float32, smallest / len(cuts), largest / len(cuts)))
        level = level * jnp.repeat(heights, shape[position] // shards_of).reshape([-1 if axis == position else 1 for axis in range(len(shape))])
    return level


def noise(own_key, dims, spread, limit, pieces=(), kind=jnp.bfloat16):
    level = block_levels(own_key, dims, pieces, -0.22, 0.18) if pieces else 1.0
    result = jax.random.normal(own_key, dims, jnp.float32) * spread * level
    return jnp.minimum(jnp.maximum(result, -limit), limit).astype(kind)


def heavy_noise(rng, extent, spread, limit, pieces, heavy, held_as=jnp.bfloat16):
    entries = spread * jax.random.normal(rng, extent, jnp.float32)
    if pieces:
        entries = entries * block_levels(rng, extent, pieces, -0.22, 0.18)
    return jnp.clip(raised(entries, jax.random.fold_in(rng, 3), *heavy), -limit, limit).astype(held_as)


def setup_inputs(seed: int = 0) -> dict:
    key_of = jax.random.split(jax.random.key(seed), 7)
    inputs = noise(key_of[0], (TOKENS, D), 1.0, 6.0, ((0, 32), (1, 4)))
    gate_preact = noise(key_of[1], (TOKENS, FF), 1.0, 6.0, ((0, 32), (1, 4)))
    hidden_grad = heavy_noise(key_of[2], (TOKENS, FF), (TOKENS ** -0.5), 0.109375, ((0, 32), (1, 4)), (0, 1, 32, 2.75))
    projector = noise(key_of[3], (D, RANK), D ** -0.5, 0.0625, ((0, 4),))
    first_moment = noise(key_of[4], (FF, RANK), 0.1, 0.6, ((0, 128),), jnp.float32)
    second_moment = jnp.clip(jnp.exp(math.log(0.1) - 2.3025851 * jax.random.uniform(key_of[5], (FF, RANK), jnp.float32) ** block_levels(key_of[5], (FF, RANK), ((0, 128),), -0.2, 0.2)), 0.01, 0.1)
    return {"inputs": inputs, "gate_preact": gate_preact, "hidden_grad": hidden_grad, "projector": projector, "first_moment": first_moment, "second_moment": second_moment}


def reference(inputs, gate_preact, hidden_grad, projector, first_moment, second_moment):
    grad_up = (hidden_grad.astype(jnp.float32) * jax.nn.silu(gate_preact.astype(jnp.float32))).astype(jnp.bfloat16)
    coords = jnp.dot(inputs, projector, preferred_element_type=jnp.float32).astype(jnp.bfloat16)
    projected = jnp.dot(grad_up.T, coords, preferred_element_type=jnp.float32)
    new_first = 0.9 * first_moment + 0.1 * projected
    new_second = 0.95 * second_moment + 0.05 * projected * projected
    direction = new_first / (1.0 - 0.81) / (jnp.sqrt(new_second / (1.0 - 0.9025)) + 1e-08)
    direction = direction.astype(jnp.bfloat16)
    update = 4.0 * jnp.dot(direction, projector.T, preferred_element_type=jnp.float32)
    return (new_first, new_second, update.astype(jnp.bfloat16))
```

```python
import jax
import jax.numpy as jnp
from jax import lax
from jax.experimental import pallas as pl
from jax.experimental.pallas import tpu as pltpu
from jax.sharding import Mesh, PartitionSpec as P


F32 = jnp.float32
BF16 = jnp.bfloat16
SIZE = {"x": 4, "z": 4, "yl": 2, "yh": 2, "c": 2}
VMEM_LIMIT = 56 * 1024 * 1024


def shift(a, axis, k):
    n = SIZE[axis]
    return lax.ppermute(a, axis, [(i, (i + k) % n) for i in range(n)])


def coords_kernel(s_ref, x_ref, w_ref, mine_ref, theirs_ref):
    c = s_ref[0]
    for out, half in ((mine_ref, c), (theirs_ref, 1 - c)):
        start = pl.multiple_of(half * 256, 256)
        out[...] = jnp.dot(x_ref[...], w_ref[:, pl.ds(start, 256)], preferred_element_type=F32)


def partial_coords(c, x, w):
    t = x.shape[0]
    return pl.pallas_call(
        coords_kernel,
        in_specs=[
            pl.BlockSpec(memory_space=pltpu.SMEM),
            pl.BlockSpec(memory_space=pltpu.VMEM),
            pl.BlockSpec(memory_space=pltpu.VMEM),
        ],
        out_shape=[jax.ShapeDtypeStruct((t, 256), F32)] * 2,
        compiler_params=pltpu.CompilerParams(vmem_limit_bytes=VMEM_LIMIT),
        name="coords",
    )(c.reshape(1), x, w)


def grad_kernel(s_ref, g_ref, h_ref, *rest):
    to_x, to_z, t_ref = rest[:4], rest[4:8], rest[8]
    i = pl.program_id(0)
    xp = lax.rem(s_ref[0] + i, 4)

    @pl.loop(0, 14)
    def _(b):
        cols = pl.ds(pl.multiple_of(b * 128, 128), 128)
        v = g_ref[:, cols].astype(F32)
        h = h_ref[:, cols].astype(F32)
        u = (h * (v / (1.0 + jnp.exp(-v)))).astype(BF16)
        t_ref[cols, :] = u.T

    for j in range(4):

        @pl.when(i == j)
        def _():
            for q in range(4):
                to_x[j][q] = t_ref[q * 448 : q * 448 + 224, :]

    for k in range(4):
        start = pl.multiple_of(lax.rem(s_ref[1] + k, 4) * 448 + 224, 224)
        to_z[k][xp] = t_ref[pl.ds(start, 224), :]


def grad_pieces(xz, gate, hidden):
    t = gate.shape[0]
    spec = pl.BlockSpec((t, 1792), lambda i, s: (0, lax.rem(s[0] + i, 4)))
    return pl.pallas_call(
        grad_kernel,
        grid_spec=pltpu.PrefetchScalarGridSpec(
            num_scalar_prefetch=1,
            grid=(4,),
            in_specs=[spec, spec],
            out_specs=[pl.BlockSpec((4, 224, t), lambda i, s: (0, 0, 0))] * 8,
            scratch_shapes=[pltpu.VMEM((1792, t), BF16)],
        ),
        out_shape=[jax.ShapeDtypeStruct((4, 224, t), BF16)] * 8,
        compiler_params=pltpu.CompilerParams(vmem_limit_bytes=VMEM_LIMIT),
        name="grads",
    )(xz, gate, hidden)


def matmul_kernel(picks, s_ref, g0, g1, g2, g3, own_ref, other_ref, o0, o1, o2, o3):
    for k, out in enumerate((o0, o1, o2, o3)):
        q = lax.rem(s_ref[0] + k, 4)
        for half, cref in enumerate((own_ref, other_ref)):
            acc = jnp.zeros((224, 256), F32)
            for g, p in zip((g0, g1, g2, g3), picks):
                acc += jnp.dot(g[q], cref[p], preferred_element_type=F32)
            out[:, half * 256 : half * 256 + 256] = acc.astype(out.dtype)


def partial_sums(picks, at, pieces, own, other):
    return pl.pallas_call(
        lambda *refs: matmul_kernel(picks, *refs),
        in_specs=[pl.BlockSpec(memory_space=pltpu.SMEM)]
        + [pl.BlockSpec(memory_space=pltpu.VMEM)] * 6,
        out_shape=[jax.ShapeDtypeStruct((224, 512), F32)]
        + [jax.ShapeDtypeStruct((224, 512), BF16)] * 3,
        compiler_params=pltpu.CompilerParams(vmem_limit_bytes=VMEM_LIMIT),
        name="matmul",
    )(at.reshape(1), *pieces, own, other)


def step(inputs, gate_preact, hidden_grad, projector, first_moment, second_moment):
    x, z, yl, yh, c = (lax.axis_index(a).astype(jnp.int32) for a in ("x", "z", "yl", "yh", "c"))

    mine, theirs = partial_coords(c, inputs, projector)
    theirs = shift(theirs, "c", 1)
    pieces = grad_pieces(jnp.stack([x, z]), gate_preact, hidden_grad)
    theirs, pieces = lax.optimization_barrier((theirs, pieces))
    from_x = [pieces[0]] + [shift(pieces[k], "x", k) for k in (1, 2, 3)]
    from_z = [pieces[4]] + [shift(pieces[4 + k], "z", k) for k in (1, 2, 3)]

    chip_sum = mine + theirs
    far = shift(chip_sum.astype(BF16), "yh", 1)
    half = (chip_sum + far.astype(F32)).astype(BF16)
    own = jnp.stack(
        [half]
        + [shift(half, "x", k) for k in (1, 2, 3)]
        + [shift(half, "z", k) for k in (1, 2, 3)]
    )
    other = shift(own, "c", 1)

    beside_w = shift(projector, "c", 1)
    near_w = lax.ppermute(projector, ("yl", "yh"), [(0, 3), (3, 0), (1, 2), (2, 1)])
    across_w = shift(near_w, "c", 1)
    full_proj = jnp.zeros((4, 2048, 512), BF16)
    for at, block in (
        (2 * yh + c, projector),
        (2 * yh + 1 - c, beside_w),
        (2 - 2 * yh + c, near_w),
        (3 - 2 * yh - c, across_w),
    ):
        full_proj = lax.dynamic_update_slice(full_proj, block[None], (at, 0, 0))
    full_proj = full_proj.reshape(8192, 512)

    part_x = partial_sums((0, 1, 2, 3), z, from_x, own, other)
    part_z = partial_sums((0, 4, 5, 6), x, from_z, own, other)
    sum_x = part_x[0]
    sum_z = part_z[0]
    for k in (1, 2, 3):
        sum_x += shift(part_x[k], "z", k).astype(F32)
        sum_z += shift(part_z[k], "x", k).astype(F32)
    keep = jnp.where(yl == 0, sum_x, sum_z)
    give = jnp.where(yl == 0, sum_z, sum_x).astype(BF16)
    total = keep + shift(give, "yl", 1).astype(F32)
    swapped = jnp.concatenate([total[:, 256:], total[:, :256]], axis=1)
    projected = jnp.where(c == 0, total, swapped)

    new_first = 0.9 * first_moment + 0.1 * projected
    new_second = 0.95 * second_moment + 0.05 * projected * projected
    direction = new_first / (1.0 - 0.81) / (jnp.sqrt(new_second / (1.0 - 0.9025)) + 1e-08)
    direction = direction.astype(BF16)
    update = 4.0 * lax.dot_general(
        direction, full_proj, (((1,), (1,)), ((), ())), preferred_element_type=F32
    )
    return (new_first, new_second, update.astype(BF16))


def solution(mesh):
    fine = Mesh(mesh.devices.reshape(4, 4, 2, 2, 2), ("x", "z", "yl", "yh", "c"))
    dp, mp = ("x", "z", "yl"), ("yh", "c")
    return jax.shard_map(
        step,
        mesh=fine,
        in_specs=(P(dp, mp), P(dp, mp), P(dp, mp), P(mp, None), P(mp + dp, None), P(mp + dp, None)),
        out_specs=(P(mp + dp, None),) * 3,
        check_vma=False,
    )
```

```python
import jax
import jax.numpy as jnp
from jax import lax
from jax.experimental import pallas as pl
from jax.experimental.pallas import tpu as pltpu
from jax.sharding import Mesh, PartitionSpec as P


F32 = jnp.float32
BF16 = jnp.bfloat16
SIZE = {"x": 4, "z": 4, "yl": 2, "yh": 2, "c": 2}
SMEM = pl.BlockSpec(memory_space=pltpu.SMEM)
VMEM = pl.BlockSpec(memory_space=pltpu.VMEM)
HBM = pl.BlockSpec(memory_space=pl.ANY)
AXES = ("x", "z", "yl", "yh", "c")


def params(mib):
    return pltpu.CompilerParams(vmem_limit_bytes=mib * 1024 * 1024)


def shift(a, axis, k):
    n = SIZE[axis]
    return lax.ppermute(a, axis, [(i, (i + k) % n) for i in range(n)])


def cross(a, k):
    pairs = []
    for i in range(128):
        x, z, rest = i // 32, i // 8 % 4, i % 8
        if i % 2 == 0:
            x = (x + k) % 4
        else:
            z = (z + k) % 4
        pairs.append((i, x * 32 + z * 8 + rest))
    return lax.ppermute(a, AXES, pairs)


def coords_kernel(s_ref, x_ref, w_ref, mine_ref, theirs_ref):
    first = pl.program_id(0) == 0
    c = s_ref[0]
    for out, half in ((mine_ref, c), (theirs_ref, 1 - c)):
        start = pl.multiple_of(half * 256, 256)
        part = jnp.dot(x_ref[...], w_ref[:, pl.ds(start, 256)], preferred_element_type=F32)
        out[...] = jnp.where(first, part, out[...] + part)


def partial_coords(c, x, w):
    t = x.shape[0]
    return pl.pallas_call(
        coords_kernel,
        grid=(4,),
        in_specs=[
            SMEM,
            pl.BlockSpec((t, 512), lambda i: (0, i)),
            pl.BlockSpec((512, 512), lambda i: (i, 0)),
        ],
        out_specs=[VMEM] * 2,
        out_shape=[pltpu.VMEM((t, 256), F32)] * 2,
        compiler_params=params(8),
        name="coords",
    )(c.reshape(1), x, w)


def grad_kernel(s_ref, g_ref, h_ref, x0, x1, x2, x3, z0, z1, z2, z3, t_ref):
    i = pl.program_id(0)
    for b in range(14):
        cols = slice(b * 128, b * 128 + 128)
        v = 0.5 * g_ref[:, cols].astype(F32)
        w = v * h_ref[:, cols].astype(F32)
        t_ref[cols, :] = (w + w * jnp.tanh(v)).astype(BF16).T
    for k, out in enumerate((z0, z1, z2, z3)):
        start = pl.multiple_of(lax.rem(s_ref[1] + k, 4) * 448, 448)
        out[i] = t_ref[pl.ds(start + 224, 224), :]
        for j, own in enumerate((x0, x1, x2, x3)):

            @pl.when(i == j)
            def _():
                own[k] = t_ref[pl.ds(start, 224), :]


def grad_pieces(xz, gate, hidden):
    t = gate.shape[0]
    spec = pl.BlockSpec((t, 1792), lambda i, s: (0, lax.rem(s[0] + i, 4)))
    return pl.pallas_call(
        grad_kernel,
        grid_spec=pltpu.PrefetchScalarGridSpec(
            num_scalar_prefetch=1,
            grid=(4,),
            in_specs=[spec, spec],
            out_specs=[VMEM] * 8,
            scratch_shapes=[pltpu.VMEM((1792, t), BF16)],
        ),
        out_shape=[pltpu.VMEM((4, 224, t), BF16)] * 8,
        compiler_params=params(16),
        name="grads",
    )(xz, gate, hidden)


def partial_sums(near, late):
    acc = None
    for piece, coords in near:
        part = jnp.dot(piece.reshape(896, -1), coords, preferred_element_type=F32)
        acc = part if acc is None else acc + part
    acc = lax.optimization_barrier(acc)
    piece, coords = late
    out = []
    for j in range(4):
        part = jnp.dot(piece[j], coords, preferred_element_type=F32)
        part += acc[j * 224 : j * 224 + 224]
        out.append(part if j == 0 else part.astype(BF16))
    return out


def last_kernel(
    s_ref, mine, got, first, second, w0, w1, w2, w3, new_first, new_second, update, o_ref, sem
):
    yh, c = s_ref[0], s_ref[1]
    projected = mine[...] + got[...].astype(F32)
    m = 0.9 * first[...] + 0.1 * projected
    v = 0.95 * second[...] + 0.05 * projected * projected
    new_first[...] = m
    new_second[...] = v
    direction = (m / (1.0 - 0.81) / (jnp.sqrt(v / (1.0 - 0.9025)) + 1e-08)).astype(BF16)
    blocks = (2 * yh + c, 2 * yh + 1 - c, 2 - 2 * yh + c, 3 - 2 * yh - c)
    stores = []
    for k, w_ref in enumerate((w0, w1, w2, w3)):
        part = 4.0 * lax.dot_general(
            direction, w_ref[...], (((1,), (1,)), ((), ())), preferred_element_type=F32
        )
        o_ref[k] = part.astype(BF16)
        cols = pl.ds(pl.multiple_of(blocks[k] * 2048, 2048), 2048)
        store = pltpu.make_async_copy(o_ref.at[k], update.at[:, cols], sem.at[k])
        store.start()
        stores.append(store)
    for store in stores:
        store.wait()


def last_stage(at, mine, got, first, second, blocks):
    rows = first.shape[0]
    moment = jax.ShapeDtypeStruct((rows, 512), F32)
    args = [pltpu.with_memory_space_constraint(a, pltpu.VMEM) for a in (mine, got, first, second) + blocks]
    return pl.pallas_call(
        last_kernel,
        in_specs=[SMEM] + [VMEM] * 8,
        out_specs=[VMEM, VMEM, HBM],
        out_shape=[moment, moment, jax.ShapeDtypeStruct((rows, 8192), BF16)],
        scratch_shapes=[pltpu.VMEM((4, rows, 2048), BF16), pltpu.SemaphoreType.DMA((4,))],
        compiler_params=params(12),
        name="last",
    )(at, *args)


def step(inputs, gate_preact, hidden_grad, projector, first_moment, second_moment):
    x, z, yl, yh, c = (lax.axis_index(a).astype(jnp.int32) for a in AXES)
    place = jnp.stack([x, z, yh, c])

    inputs, gate_preact, hidden_grad = (
        pltpu.with_memory_space_constraint(a, pltpu.HBM) for a in (inputs, gate_preact, hidden_grad)
    )
    mine, theirs = partial_coords(
        c, inputs, pltpu.with_memory_space_constraint(projector, pltpu.HBM)
    )
    theirs = shift(theirs, "c", 1)
    chip_sum = mine + theirs
    far = shift(chip_sum.astype(BF16), "yh", 1)
    half = (chip_sum + far.astype(F32)).astype(BF16)
    other = shift(half, "c", 1)
    own = jnp.concatenate(
        [jnp.where(c == 0, half, other), jnp.where(c == 0, other, half)], axis=1
    )
    along = {k: cross(own, k) for k in (1, 3, 2)}
    beyond = {k: shift(along[k], "c", 1) for k in (1, 3, 2)}
    coords_x = {k: jnp.where(c == 0, along[k], beyond[k]) for k in (1, 3, 2)}
    coords_z = {k: jnp.where(c == 0, beyond[k], along[k]) for k in (1, 3, 2)}

    near_w = lax.ppermute(projector, ("yl", "yh"), [(0, 3), (3, 0), (1, 2), (2, 1)])
    beside_w = shift(projector, "c", 1)
    across_w = shift(near_w, "c", 1)

    pieces = grad_pieces(jnp.stack([x, z]), gate_preact, hidden_grad)
    from_x = [pieces[0]] + [shift(pieces[k], "x", k) for k in (1, 2, 3)]
    from_z = [pieces[4]] + [shift(pieces[4 + k], "z", k) for k in (1, 2, 3)]

    sums = []
    for got, coords, axis in ((from_z, coords_z, "x"), (from_x, coords_x, "z")):
        part = partial_sums(
            [(got[0], own), (got[1], coords[1]), (got[3], coords[3])], (got[2], coords[2])
        )
        total = part[0]
        for k in (1, 3, 2):
            total += shift(part[k], axis, k).astype(F32)
        sums.append(total)
    sum_z, sum_x = sums
    keep = jnp.where(yl == 0, sum_x, sum_z)
    give = jnp.where(yl == 0, sum_z, sum_x).astype(BF16)
    got = shift(give, "yl", 1)
    return last_stage(
        place[2:], keep, got, first_moment, second_moment, (projector, beside_w, near_w, across_w)
    )


def solution(mesh):
    fine = Mesh(mesh.devices.reshape(4, 4, 2, 2, 2), ("x", "z", "yl", "yh", "c"))
    dp, mp = ("x", "z", "yl"), ("yh", "c")
    return jax.shard_map(
        step,
        mesh=fine,
        in_specs=(P(dp, mp), P(dp, mp), P(dp, mp), P(mp, None), P(mp + dp, None), P(mp + dp, None)),
        out_specs=(P(mp + dp, None),) * 3,
        check_vma=False,
    )
```

```python
import jax
import jax.numpy as jnp
from jax import lax
from jax.experimental import pallas as pl
from jax.experimental.pallas import tpu as pltpu
from jax.sharding import Mesh, PartitionSpec as P


F32 = jnp.float32
BF16 = jnp.bfloat16
SIZE = {"x": 4, "z": 4, "yl": 2, "yh": 2, "c": 2}
SMEM = pl.BlockSpec(memory_space=pltpu.SMEM)
VMEM = pl.BlockSpec(memory_space=pltpu.VMEM)
HBM = pl.BlockSpec(memory_space=pl.ANY)
AXES = ("x", "z", "yl", "yh", "c")


def params(mib):
    return pltpu.CompilerParams(vmem_limit_bytes=mib * 1024 * 1024)


def shift(a, axis, k):
    n = SIZE[axis]
    return lax.ppermute(a, axis, [(i, (i + k) % n) for i in range(n)])


def cross(a, k):
    pairs = []
    for i in range(128):
        x, z, rest = i // 32, i // 8 % 4, i % 8
        if i % 2 == 0:
            x = (x + k) % 4
        else:
            z = (z + k) % 4
        pairs.append((i, x * 32 + z * 8 + rest))
    return lax.ppermute(a, AXES, pairs)


def store(whole, early, late, row, value):
    if whole is None:
        (early if row in (1, 2) else late)[{1: 0, 2: 1, 3: 0, 0: 1}[row]] = value
    else:
        whole[row] = value


def front_kernel(s_ref, g_ref, h_ref, i_ref, w_ref, mine, theirs, *rest):
    outs, t_ref = rest[:-1], rest[-1]
    to_x = (outs[0], outs[1], None, outs[2])
    to_z = (outs[5], outs[6], None, outs[7])
    i = pl.program_id(0)
    for b in range(14):
        cols = slice(b * 128, b * 128 + 128)
        v = 0.5 * g_ref[:, cols].astype(F32)
        w = v * h_ref[:, cols].astype(F32)
        t_ref[cols, :] = (w + w * jnp.tanh(v)).astype(BF16).T
    c = s_ref[2]
    for out, half in ((mine, c), (theirs, 1 - c)):
        start = pl.multiple_of(half * 256, 256)
        part = jnp.dot(i_ref[...], w_ref[:, pl.ds(start, 256)], preferred_element_type=F32)

        @pl.when(i == 0)
        def _():
            out[...] = part

        @pl.when(i > 0)
        def _():
            out[...] += part

    for k in range(4):
        start = pl.multiple_of(lax.rem(s_ref[1] + k, 4) * 448, 448)
        for j in range(4):

            @pl.when(i == j)
            def _():
                store(to_x[j], outs[3], outs[4], k, t_ref[pl.ds(start, 224), :])
                store(to_z[k], outs[8], outs[9], j, t_ref[pl.ds(start + 224, 224), :])


def front(at, gate, hidden, inputs, projector):
    t = gate.shape[0]
    block = pl.BlockSpec((t, 1792), lambda i, s: (0, lax.rem(s[0] + i, 4)))
    whole, part = pltpu.VMEM((4, 224, t), BF16), pltpu.VMEM((2, 224, t), BF16)
    args = [
        pltpu.with_memory_space_constraint(a, pltpu.HBM) for a in (gate, hidden, inputs, projector)
    ]
    return pl.pallas_call(
        front_kernel,
        grid_spec=pltpu.PrefetchScalarGridSpec(
            num_scalar_prefetch=1,
            grid=(4,),
            in_specs=[
                block,
                block,
                pl.BlockSpec((t, 512), lambda i, s: (0, i)),
                pl.BlockSpec((512, 512), lambda i, s: (i, 0)),
            ],
            out_specs=[VMEM] * 12,
            scratch_shapes=[pltpu.VMEM((1792, t), BF16)],
        ),
        out_shape=[pltpu.VMEM((t, 256), F32)] * 2 + [whole, whole, whole, part, part] * 2,
        compiler_params=params(16),
        name="front",
    )(at, *args)


def join_kernel(s_ref, half, other, out):
    c = s_ref[2]
    out[:, pl.ds(pl.multiple_of(c * 256, 256), 256)] = half[...]
    out[:, pl.ds(pl.multiple_of(256 - c * 256, 256), 256)] = other[...]


def join(at, half, other):
    args = [pltpu.with_memory_space_constraint(a, pltpu.VMEM) for a in (half, other)]
    return pl.pallas_call(
        join_kernel,
        in_specs=[SMEM, VMEM, VMEM],
        out_specs=VMEM,
        out_shape=pltpu.VMEM((half.shape[0], 512), BF16),
        compiler_params=params(4),
        name="join",
    )(at, *args)


def hold_kernel(a, b, c, x, y, z, sem):
    copies = [pltpu.make_async_copy(s, d, sem.at[k]) for k, (s, d) in enumerate(((a, x), (b, y), (c, z)))]
    for copy in copies:
        copy.start()
    for copy in copies:
        copy.wait()


def hold(blocks):
    args = [pltpu.with_memory_space_constraint(a, pltpu.HBM) for a in blocks]
    return pl.pallas_call(
        hold_kernel,
        in_specs=[HBM] * 3,
        out_specs=[VMEM] * 3,
        out_shape=[pltpu.VMEM((2048, 512), BF16)] * 3,
        scratch_shapes=[pltpu.SemaphoreType.DMA((3,))],
        compiler_params=params(1),
        name="keep",
    )(*args)


def partial_sums(near, late):
    acc = None
    for piece, coords in near:
        part = jnp.dot(piece.reshape(896, -1), coords, preferred_element_type=F32)
        acc = part if acc is None else acc + part
    acc = lax.optimization_barrier(acc)
    (first, second), coords = late
    rows = {1: first[0], 2: first[1], 3: second[0], 0: second[1]}
    out = {}
    for j in (1, 2, 3, 0):
        part = jnp.dot(rows[j], coords, preferred_element_type=F32)
        part += acc[j * 224 : j * 224 + 224]
        out[j] = part if j == 0 else part.astype(BF16)
    return out


def last_kernel(
    s_ref, mine, got, first, second, w0, w1, w2, w3, new_first, new_second, update,
    w_ref, o_ref, sem, w_sem,
):
    yh, c = s_ref[3], s_ref[2]
    load = pltpu.make_async_copy(w3, w_ref, w_sem)
    load.start()
    projected = mine[...] + got[...].astype(F32)
    m = 0.9 * first[...] + 0.1 * projected
    v = 0.95 * second[...] + 0.05 * projected * projected
    new_first[...] = m
    new_second[...] = v
    root = jnp.sqrt(v * (1.0 / (1.0 - 0.9025)))
    direction = (m * (1.0 / (1.0 - 0.81)) / (root + 1e-08)).astype(BF16)
    blocks = (2 * yh + c, 2 * yh + 1 - c, 2 - 2 * yh + c, 3 - 2 * yh - c)
    stores = []
    for k, w in enumerate((w0, w1, w2, w_ref)):
        if k == 3:
            load.wait()
        part = 4.0 * lax.dot_general(
            direction, w[...], (((1,), (1,)), ((), ())), preferred_element_type=F32
        )
        o_ref[k] = part.astype(BF16)
        cols = pl.ds(pl.multiple_of(blocks[k] * 2048, 2048), 2048)
        out = pltpu.make_async_copy(o_ref.at[k], update.at[:, cols], sem.at[k])
        out.start()
        stores.append(out)
    for out in stores:
        out.wait()


def last_stage(at, mine, got, first, second, held, across):
    rows = first.shape[0]
    moment = jax.ShapeDtypeStruct((rows, 512), F32)
    args = [
        pltpu.with_memory_space_constraint(a, pltpu.VMEM)
        for a in (mine, got, first, second) + tuple(held)
    ]
    return pl.pallas_call(
        last_kernel,
        in_specs=[SMEM] + [VMEM] * 7 + [HBM],
        out_specs=[VMEM, VMEM, HBM],
        out_shape=[moment, moment, jax.ShapeDtypeStruct((rows, 8192), BF16)],
        scratch_shapes=[
            pltpu.VMEM((2048, 512), BF16),
            pltpu.VMEM((4, rows, 2048), BF16),
            pltpu.SemaphoreType.DMA((4,)),
            pltpu.SemaphoreType.DMA,
        ],
        compiler_params=params(12),
        name="last",
    )(at, *args, pltpu.with_memory_space_constraint(across, pltpu.HBM))


def step(inputs, gate_preact, hidden_grad, projector, first_moment, second_moment):
    x, z, yl, yh, c = (lax.axis_index(a).astype(jnp.int32) for a in AXES)
    at = jnp.stack([x, z, c, yh])

    mine, theirs, *pieces = front(at, gate_preact, hidden_grad, inputs, projector)
    got_x, got_z = {}, {}
    for got, parts, axis in ((got_x, pieces[:5], "x"), (got_z, pieces[5:], "z")):
        got[0] = parts[0]
        for key, k, part in (("1", 1, parts[1]), ("3", 3, parts[2]), ("2a", 2, parts[3]), ("2b", 2, parts[4])):
            got[key] = shift(part, axis, k)

    chip_sum = mine + shift(theirs, "c", 1)
    far = shift(chip_sum.astype(BF16), "yh", 1)
    half = (chip_sum + far.astype(F32)).astype(BF16)
    own = join(at, half, shift(half, "c", 1))
    along = {k: cross(own, k) for k in (1, 3, 2)}
    beyond = {k: shift(along[k], "c", 1) for k in (1, 3, 2)}
    coords_x = {k: jnp.where(c == 0, along[k], beyond[k]) for k in (1, 3, 2)}
    coords_z = {k: jnp.where(c == 0, beyond[k], along[k]) for k in (1, 3, 2)}

    near_w = lax.ppermute(projector, ("yl", "yh"), [(0, 3), (3, 0), (1, 2), (2, 1)])
    beside_w = shift(projector, "c", 1)
    across_w = shift(near_w, "c", 1)

    sums = []
    for got, coords, axis in ((got_z, coords_z, "x"), (got_x, coords_x, "z")):
        part = partial_sums(
            [(got[0], own), (got["1"], coords[1]), (got["3"], coords[3])],
            ((got["2a"], got["2b"]), coords[2]),
        )
        total = part[0]
        for k in (1, 2, 3):
            total += shift(part[k], axis, k).astype(F32)
        sums.append(total)
    sum_z, sum_x = sums
    keep = jnp.where(yl == 0, sum_x, sum_z)
    give = jnp.where(yl == 0, sum_z, sum_x).astype(BF16)
    got = shift(give, "yl", 1)
    held = hold((projector, beside_w, near_w))
    return last_stage(at, keep, got, first_moment, second_moment, held, across_w)


def solution(mesh):
    fine = Mesh(mesh.devices.reshape(4, 4, 2, 2, 2), ("x", "z", "yl", "yh", "c"))
    dp, mp = ("x", "z", "yl"), ("yh", "c")
    return jax.shard_map(
        step,
        mesh=fine,
        in_specs=(P(dp, mp), P(dp, mp), P(dp, mp), P(mp, None), P(mp + dp, None), P(mp + dp, None)),
        out_specs=(P(mp + dp, None),) * 3,
        check_vma=False,
    )
```

```python
import jax
import jax.numpy as jnp
from jax import lax
from jax.experimental import pallas as pl
from jax.experimental.pallas import tpu as pltpu
from jax.sharding import Mesh, PartitionSpec as P


F32 = jnp.float32
BF16 = jnp.bfloat16
SIZE = {"x": 4, "z": 4, "yl": 2, "yh": 2, "c": 2}
SMEM = pl.BlockSpec(memory_space=pltpu.SMEM)
VMEM = pl.BlockSpec(memory_space=pltpu.VMEM)
HBM = pl.BlockSpec(memory_space=pl.ANY)
AXES = ("x", "z", "yl", "yh", "c")


def params(mib):
    return pltpu.CompilerParams(vmem_limit_bytes=mib * 1024 * 1024)


def shift(a, axis, k):
    n = SIZE[axis]
    return lax.ppermute(a, axis, [(i, (i + k) % n) for i in range(n)])


def cross(a, k):
    pairs = []
    for i in range(128):
        x, z, rest = i // 32, i // 8 % 4, i % 8
        if i % 2 == 0:
            x = (x + k) % 4
        else:
            z = (z + k) % 4
        pairs.append((i, x * 32 + z * 8 + rest))
    return lax.ppermute(a, AXES, pairs)


def front_kernel(s_ref, g_ref, h_ref, i_ref, w_ref, mine, theirs, *rest):
    outs, t_ref = rest[:-1], rest[-1]
    to_x, to_z = outs[:4], outs[4:]
    i = pl.program_id(0)
    for b in range(14):
        cols = slice(b * 128, b * 128 + 128)
        v = 0.5 * g_ref[:, cols].astype(F32)
        w = v * h_ref[:, cols].astype(F32)
        t_ref[cols, :] = (w + w * jnp.tanh(v)).astype(BF16).T
    c = s_ref[2]
    for out, half in ((mine, c), (theirs, 1 - c)):
        start = pl.multiple_of(half * 256, 256)
        part = jnp.dot(i_ref[...], w_ref[:, pl.ds(start, 256)], preferred_element_type=F32)

        @pl.when(i == 0)
        def _():
            out[...] = part

        @pl.when(i > 0)
        def _():
            out[...] += part

    for k in range(4):
        start = pl.multiple_of(lax.rem(s_ref[1] + k, 4) * 448, 448)
        to_z[k][i] = t_ref[pl.ds(start + 224, 224), :]
        for j in range(4):

            @pl.when(i == j)
            def _():
                to_x[j][k] = t_ref[pl.ds(start, 224), :]


def front(at, gate, hidden, inputs, projector):
    t = gate.shape[0]
    block = pl.BlockSpec((t, 1792), lambda i, s: (0, lax.rem(s[0] + i, 4)))
    args = [
        pltpu.with_memory_space_constraint(a, pltpu.HBM) for a in (gate, hidden, inputs, projector)
    ]
    return pl.pallas_call(
        front_kernel,
        grid_spec=pltpu.PrefetchScalarGridSpec(
            num_scalar_prefetch=1,
            grid=(4,),
            in_specs=[
                block,
                block,
                pl.BlockSpec((t, 512), lambda i, s: (0, i)),
                pl.BlockSpec((512, 512), lambda i, s: (i, 0)),
            ],
            out_specs=[VMEM] * 10,
            scratch_shapes=[pltpu.VMEM((1792, t), BF16)],
        ),
        out_shape=[pltpu.VMEM((t, 256), F32)] * 2 + [pltpu.VMEM((4, 224, t), BF16)] * 8,
        compiler_params=params(16),
        name="front",
    )(at, *args)


def join_kernel(s_ref, half, other, out):
    c = s_ref[2]
    out[:, pl.ds(pl.multiple_of(c * 256, 256), 256)] = half[...]
    out[:, pl.ds(pl.multiple_of(256 - c * 256, 256), 256)] = other[...]


def join(at, half, other):
    args = [pltpu.with_memory_space_constraint(a, pltpu.VMEM) for a in (half, other)]
    return pl.pallas_call(
        join_kernel,
        in_specs=[SMEM, VMEM, VMEM],
        out_specs=VMEM,
        out_shape=pltpu.VMEM((half.shape[0], 512), BF16),
        compiler_params=params(4),
        name="join",
    )(at, *args)


def hold_kernel(a, b, c, x, y, z, sem):
    copies = [pltpu.make_async_copy(s, d, sem.at[k]) for k, (s, d) in enumerate(((a, x), (b, y), (c, z)))]
    for copy in copies:
        copy.start()
    for copy in copies:
        copy.wait()


def hold(blocks):
    args = [pltpu.with_memory_space_constraint(a, pltpu.HBM) for a in blocks]
    return pl.pallas_call(
        hold_kernel,
        in_specs=[HBM] * 3,
        out_specs=[VMEM] * 3,
        out_shape=[pltpu.VMEM((2048, 512), BF16)] * 3,
        scratch_shapes=[pltpu.SemaphoreType.DMA((3,))],
        compiler_params=params(1),
        name="keep",
    )(*args)


def early_kernel(s_ref, g0, g1, g3, c0, along1, beyond1, along3, beyond3, out, rhs):
    q = pl.program_id(0)

    @pl.when(q == 0)
    def _():
        rhs[0:384, :] = c0[...]

    for pick, ones, threes in ((0, along1, along3), (1, beyond1, beyond3)):

        @pl.when((q == 0) & (s_ref[0] == pick))
        def _():
            rhs[384:768, :] = ones[...]
            rhs[768:1152, :] = threes[...]

    lhs = jnp.concatenate([g0[0], g1[0], g3[0]], axis=1)
    out[q] = jnp.dot(lhs, rhs[...], preferred_element_type=F32)


def early_sums(pick, pieces, coords):
    t = pieces[0].shape[-1]
    piece = pl.BlockSpec((1, 224, t), lambda q, s: (q, 0, 0))
    whole = pl.BlockSpec((t, 512), lambda q, s: (0, 0))
    return pl.pallas_call(
        early_kernel,
        grid_spec=pltpu.PrefetchScalarGridSpec(
            num_scalar_prefetch=1,
            grid=(4,),
            in_specs=[piece] * 3 + [whole] * 5,
            out_specs=VMEM,
            scratch_shapes=[pltpu.VMEM((3 * t, 512), BF16)],
        ),
        out_shape=pltpu.VMEM((4, 224, 512), F32),
        compiler_params=params(10),
    )(pick.reshape(1), *pieces, *coords)


def late_kernel(s_ref, acc, g2, along, beyond, o0, o1, o2, o3, rhs):
    for pick, ref in ((0, along), (1, beyond)):

        @pl.when(s_ref[0] == pick)
        def _():
            rhs[...] = ref[...]

    for j, out in enumerate((o0, o1, o2, o3)):
        part = acc[j] + jnp.dot(g2[j], rhs[...], preferred_element_type=F32)
        out[...] = part.astype(out.dtype)


def late_sums(pick, acc, piece, coords):
    t = piece.shape[-1]
    return pl.pallas_call(
        late_kernel,
        in_specs=[SMEM] + [VMEM] * 4,
        out_specs=[VMEM] * 4,
        out_shape=[pltpu.VMEM((224, 512), F32)] + [pltpu.VMEM((224, 512), BF16)] * 3,
        scratch_shapes=[pltpu.VMEM((t, 512), BF16)],
        compiler_params=params(6),
    )(pick.reshape(1), pltpu.with_memory_space_constraint(acc, pltpu.VMEM), piece, *coords)


def combine_kernel(s_ref, x0, x1, x2, x3, z0, z1, z2, z3, keep, give):
    sum_x = x0[...] + x1[...].astype(F32) + x2[...].astype(F32) + x3[...].astype(F32)
    sum_z = z0[...] + z1[...].astype(F32) + z2[...].astype(F32) + z3[...].astype(F32)
    here = s_ref[0] == 0
    keep[...] = jnp.where(here, sum_x, sum_z)
    give[...] = jnp.where(here, sum_z, sum_x).astype(BF16)


def combine(yl, parts_x, parts_z):
    own = [pltpu.with_memory_space_constraint(p[0], pltpu.VMEM) for p in (parts_x, parts_z)]
    return pl.pallas_call(
        combine_kernel,
        in_specs=[SMEM] + [VMEM] * 8,
        out_specs=[VMEM] * 2,
        out_shape=[pltpu.VMEM((224, 512), F32), pltpu.VMEM((224, 512), BF16)],
        compiler_params=params(4),
        name="combine",
    )(yl.reshape(1), own[0], *parts_x[1:], own[1], *parts_z[1:])


def last_kernel(
    s_ref, mine, got, first, second, w0, w1, w2, w3, new_first, new_second, update,
    w_ref, o_ref, sem, w_sem,
):
    yh, c = s_ref[3], s_ref[2]
    load = pltpu.make_async_copy(w3, w_ref, w_sem)
    load.start()
    projected = mine[...] + got[...].astype(F32)
    m = 0.9 * first[...] + 0.1 * projected
    v = 0.95 * second[...] + 0.05 * projected * projected
    new_first[...] = m
    new_second[...] = v
    root = jnp.sqrt(v * (1.0 / (1.0 - 0.9025)))
    direction = (m * (1.0 / (1.0 - 0.81)) / (root + 1e-08)).astype(BF16)
    blocks = (2 * yh + c, 2 * yh + 1 - c, 2 - 2 * yh + c, 3 - 2 * yh - c)
    stores = []
    for k, w in enumerate((w0, w1, w2, w_ref)):
        if k == 3:
            load.wait()
        part = 4.0 * lax.dot_general(
            direction, w[...], (((1,), (1,)), ((), ())), preferred_element_type=F32
        )
        o_ref[k] = part.astype(BF16)
        cols = pl.ds(pl.multiple_of(blocks[k] * 2048, 2048), 2048)
        out = pltpu.make_async_copy(o_ref.at[k], update.at[:, cols], sem.at[k])
        out.start()
        stores.append(out)
    for out in stores:
        out.wait()


def last_stage(at, mine, got, first, second, held, across):
    rows = first.shape[0]
    moment = jax.ShapeDtypeStruct((rows, 512), F32)
    args = [
        pltpu.with_memory_space_constraint(a, pltpu.VMEM)
        for a in (mine, got, first, second) + tuple(held)
    ]
    return pl.pallas_call(
        last_kernel,
        in_specs=[SMEM] + [VMEM] * 7 + [HBM],
        out_specs=[VMEM, VMEM, HBM],
        out_shape=[moment, moment, jax.ShapeDtypeStruct((rows, 8192), BF16)],
        scratch_shapes=[
            pltpu.VMEM((2048, 512), BF16),
            pltpu.VMEM((4, rows, 2048), BF16),
            pltpu.SemaphoreType.DMA((4,)),
            pltpu.SemaphoreType.DMA,
        ],
        compiler_params=params(12),
        name="last",
    )(at, *args, pltpu.with_memory_space_constraint(across, pltpu.HBM))


def step(inputs, gate_preact, hidden_grad, projector, first_moment, second_moment):
    x, z, yl, yh, c = (lax.axis_index(a).astype(jnp.int32) for a in AXES)
    at = jnp.stack([x, z, c, yh])

    mine, theirs, *pieces = front(at, gate_preact, hidden_grad, inputs, projector)
    got_x = [pieces[0]] + [shift(pieces[k], "x", k) for k in (1, 2, 3)]
    got_z = [pieces[4]] + [shift(pieces[4 + k], "z", k) for k in (1, 2, 3)]

    chip_sum = mine + shift(theirs, "c", 1)
    far = shift(chip_sum.astype(BF16), "yh", 1)
    half = (chip_sum + far.astype(F32)).astype(BF16)
    own = join(at, half, shift(half, "c", 1))
    along = {k: cross(own, k) for k in (1, 3, 2)}
    beyond = {k: shift(along[k], "c", 1) for k in (1, 3, 2)}

    near_w = lax.ppermute(projector, ("yl", "yh"), [(0, 3), (3, 0), (1, 2), (2, 1)])
    beside_w = shift(projector, "c", 1)
    across_w = shift(near_w, "c", 1)

    parts = []
    for got, pick, axis in ((got_z, 1 - c, "x"), (got_x, c, "z")):
        near = (own, along[1], beyond[1], along[3], beyond[3])
        acc = early_sums(pick, (got[0], got[1], got[3]), near)
        part = late_sums(pick, acc, got[2], (along[2], beyond[2]))
        parts.append([part[0]] + [shift(part[k], axis, k) for k in (1, 2, 3)])
    parts_z, parts_x = parts
    keep, give = combine(yl, parts_x, parts_z)
    got = shift(give, "yl", 1)
    held = hold((projector, beside_w, near_w))
    return last_stage(at, keep, got, first_moment, second_moment, held, across_w)


def solution(mesh):
    fine = Mesh(mesh.devices.reshape(4, 4, 2, 2, 2), ("x", "z", "yl", "yh", "c"))
    dp, mp = ("x", "z", "yl"), ("yh", "c")
    return jax.shard_map(
        step,
        mesh=fine,
        in_specs=(P(dp, mp), P(dp, mp), P(dp, mp), P(mp, None), P(mp + dp, None), P(mp + dp, None)),
        out_specs=(P(mp + dp, None),) * 3,
        check_vma=False,
    )
```

```python
import jax
import jax.numpy as jnp
from jax import lax
from jax.experimental import pallas as pl
from jax.experimental.pallas import tpu as pltpu
from jax.sharding import Mesh, PartitionSpec as P


F32 = jnp.float32
BF16 = jnp.bfloat16
SIZE = {"x": 4, "z": 4, "yl": 2, "yh": 2, "c": 2}
SMEM = pl.BlockSpec(memory_space=pltpu.SMEM)
VMEM = pl.BlockSpec(memory_space=pltpu.VMEM)
HBM = pl.BlockSpec(memory_space=pl.ANY)
AXES = ("x", "z", "yl", "yh", "c")


def params(mib):
    return pltpu.CompilerParams(vmem_limit_bytes=mib * 1024 * 1024)


def shift(a, axis, k):
    n = SIZE[axis]
    return lax.ppermute(a, axis, [(i, (i + k) % n) for i in range(n)])


def cross(a, k):
    pairs = []
    for i in range(128):
        x, z, rest = i // 32, i // 8 % 4, i % 8
        if i % 2 == 0:
            x = (x + k) % 4
        else:
            z = (z + k) % 4
        pairs.append((i, x * 32 + z * 8 + rest))
    return lax.ppermute(a, AXES, pairs)


def front_kernel(s_ref, g_ref, h_ref, i_ref, w_ref, mine, theirs, *rest):
    outs, t_ref = rest[:-1], rest[-1]
    to_x, to_z = outs[:4], outs[4:]
    i = pl.program_id(0)
    for b in range(14):
        cols = slice(b * 128, b * 128 + 128)
        v = 0.5 * g_ref[:, cols].astype(F32)
        w = v * h_ref[:, cols].astype(F32)
        t_ref[cols, :] = (w + w * jnp.tanh(v)).astype(BF16).T
    c = s_ref[2]
    for out, half in ((mine, c), (theirs, 1 - c)):
        start = pl.multiple_of(half * 256, 256)
        part = jnp.dot(i_ref[...], w_ref[:, pl.ds(start, 256)], preferred_element_type=F32)

        @pl.when(i == 0)
        def _():
            out[...] = part

        @pl.when(i > 0)
        def _():
            out[...] += part

    for k in range(4):
        start = pl.multiple_of(lax.rem(s_ref[1] + k, 4) * 448, 448)
        to_z[k][i] = t_ref[pl.ds(start + 224, 224), :]
        for j in range(4):

            @pl.when(i == j)
            def _():
                to_x[j][k] = t_ref[pl.ds(start, 224), :]


def front(at, gate, hidden, inputs, projector):
    t = gate.shape[0]
    block = pl.BlockSpec((t, 1792), lambda i, s: (0, lax.rem(s[0] + i, 4)))
    args = [
        pltpu.with_memory_space_constraint(a, pltpu.HBM) for a in (gate, hidden, inputs, projector)
    ]
    return pl.pallas_call(
        front_kernel,
        grid_spec=pltpu.PrefetchScalarGridSpec(
            num_scalar_prefetch=1,
            grid=(4,),
            in_specs=[
                block,
                block,
                pl.BlockSpec((t, 512), lambda i, s: (0, i)),
                pl.BlockSpec((512, 512), lambda i, s: (i, 0)),
            ],
            out_specs=[VMEM] * 10,
            scratch_shapes=[pltpu.VMEM((1792, t), BF16)],
        ),
        out_shape=[pltpu.VMEM((t, 256), F32)] * 2 + [pltpu.VMEM((4, 224, t), BF16)] * 8,
        compiler_params=params(16),
        name="front",
    )(at, *args)


def join_kernel(s_ref, half, other, out):
    c = s_ref[2]
    out[:, pl.ds(pl.multiple_of(c * 256, 256), 256)] = half[...]
    out[:, pl.ds(pl.multiple_of(256 - c * 256, 256), 256)] = other[...]


def join(at, half, other):
    args = [pltpu.with_memory_space_constraint(a, pltpu.VMEM) for a in (half, other)]
    return pl.pallas_call(
        join_kernel,
        in_specs=[SMEM, VMEM, VMEM],
        out_specs=VMEM,
        out_shape=pltpu.VMEM((half.shape[0], 512), BF16),
        compiler_params=params(4),
        name="join",
    )(at, *args)


def hold_kernel(a, b, x, y, sem):
    copies = []
    for k, (src, dst) in enumerate(((a, x), (b, y))):
        for q in range(2):
            rows = pl.ds(q * 1024, 1024)
            copies.append(pltpu.make_async_copy(src.at[rows], dst.at[rows], sem.at[2 * k + q]))
    for copy in copies:
        copy.start()
    for copy in copies:
        copy.wait()


def hold(blocks):
    args = [pltpu.with_memory_space_constraint(a, pltpu.HBM) for a in blocks]
    return pl.pallas_call(
        hold_kernel,
        in_specs=[HBM] * 2,
        out_specs=[VMEM] * 2,
        out_shape=[pltpu.VMEM((2048, 512), BF16)] * 2,
        scratch_shapes=[pltpu.SemaphoreType.DMA((4,))],
        compiler_params=params(1),
        name="keep",
    )(*args)


def early_kernel(s_ref, g0, g1, g3, c0, along1, beyond1, along3, beyond3, out, rhs):
    q = pl.program_id(0)

    @pl.when(q == 0)
    def _():
        rhs[0:384, :] = c0[...]

    for pick, ones, threes in ((0, along1, along3), (1, beyond1, beyond3)):

        @pl.when((q == 0) & (s_ref[0] == pick))
        def _():
            rhs[384:768, :] = ones[...]
            rhs[768:1152, :] = threes[...]

    lhs = jnp.concatenate([g0[0], g1[0], g3[0]], axis=1)
    out[q] = jnp.dot(lhs, rhs[...], preferred_element_type=F32)


def early_sums(pick, pieces, coords):
    t = pieces[0].shape[-1]
    piece = pl.BlockSpec((1, 224, t), lambda q, s: (q, 0, 0))
    whole = pl.BlockSpec((t, 512), lambda q, s: (0, 0))
    return pl.pallas_call(
        early_kernel,
        grid_spec=pltpu.PrefetchScalarGridSpec(
            num_scalar_prefetch=1,
            grid=(4,),
            in_specs=[piece] * 3 + [whole] * 5,
            out_specs=VMEM,
            scratch_shapes=[pltpu.VMEM((3 * t, 512), BF16)],
        ),
        out_shape=pltpu.VMEM((4, 224, 512), F32),
        compiler_params=params(10),
    )(pick.reshape(1), *pieces, *coords)


def late_kernel(s_ref, acc, along, beyond, g2, o0, o1, o2, o3, rhs, lhs, sem):
    order = (1, 3, 2, 0)
    loads = {j: pltpu.make_async_copy(g2.at[j], lhs.at[j], sem.at[j]) for j in order}
    for j in order:
        loads[j].start()
    for pick, ref in ((0, along), (1, beyond)):

        @pl.when(s_ref[0] == pick)
        def _():
            rhs[...] = ref[...]

    for j in order:
        out = (o0, o1, o2, o3)[j]
        loads[j].wait()
        part = acc[j] + jnp.dot(lhs[j], rhs[...], preferred_element_type=F32)
        out[...] = part.astype(out.dtype)


def late_sums(pick, acc, piece, coords):
    t = piece.shape[-1]
    args = [pltpu.with_memory_space_constraint(a, pltpu.VMEM) for a in (acc,) + coords]
    return pl.pallas_call(
        late_kernel,
        in_specs=[SMEM] + [VMEM] * 3 + [HBM],
        out_specs=[VMEM] * 4,
        out_shape=[pltpu.VMEM((224, 512), F32)] + [pltpu.VMEM((224, 512), BF16)] * 3,
        scratch_shapes=[
            pltpu.VMEM((t, 512), BF16),
            pltpu.VMEM((4, 224, t), BF16),
            pltpu.SemaphoreType.DMA((4,)),
        ],
        compiler_params=params(6),
    )(pick.reshape(1), *args, pltpu.with_memory_space_constraint(piece, pltpu.HBM))


def combine_kernel(s_ref, x0, x1, x2, x3, z0, z1, z2, z3, keep, give):
    sum_x = x0[...] + x1[...].astype(F32) + x2[...].astype(F32) + x3[...].astype(F32)
    sum_z = z0[...] + z1[...].astype(F32) + z2[...].astype(F32) + z3[...].astype(F32)
    here = s_ref[0] == 0
    keep[...] = jnp.where(here, sum_x, sum_z)
    give[...] = jnp.where(here, sum_z, sum_x).astype(BF16)


def combine(yl, parts_x, parts_z):
    own = [pltpu.with_memory_space_constraint(p[0], pltpu.VMEM) for p in (parts_x, parts_z)]
    return pl.pallas_call(
        combine_kernel,
        in_specs=[SMEM] + [VMEM] * 8,
        out_specs=[VMEM] * 2,
        out_shape=[pltpu.VMEM((224, 512), F32), pltpu.VMEM((224, 512), BF16)],
        compiler_params=params(4),
        name="combine",
    )(yl.reshape(1), own[0], *parts_x[1:], own[1], *parts_z[1:])


def last_kernel(
    s_ref, mine, got, first, second, w0, w1, w2, w3, new_first, new_second, update,
    w_ref, m_ref, o_ref, w_sem, m_sem, o_sem,
):
    yh, c = s_ref[3], s_ref[2]
    loads = []
    for k, w in enumerate((w2, w3)):
        for q in range(2):
            rows = pl.ds(q * 1024, 1024)
            loads.append(pltpu.make_async_copy(w.at[rows], w_ref.at[k, rows], w_sem.at[2 * k + q]))
    for load in loads:
        load.start()
    projected = mine[...] + got[...].astype(F32)
    m = 0.9 * first[...] + 0.1 * projected
    v = 0.95 * second[...] + 0.05 * projected * projected
    m_ref[0] = m
    m_ref[1] = v
    stores = [
        pltpu.make_async_copy(m_ref.at[k], out, m_sem.at[k])
        for k, out in enumerate((new_first, new_second))
    ]
    for out in stores:
        out.start()
    root = jnp.sqrt(v * (1.0 / (1.0 - 0.9025)))
    direction = (m * (1.0 / (1.0 - 0.81)) / (root + 1e-08)).astype(BF16)
    blocks = (2 * yh + c, 2 * yh + 1 - c, 2 - 2 * yh + c, 3 - 2 * yh - c)
    for k, w in enumerate((w0, w1, w_ref.at[0], w_ref.at[1])):
        for q in range(2):
            if k >= 2:
                loads[2 * k - 4 + q].wait()
            part = 4.0 * lax.dot_general(
                direction,
                w[q * 1024 : q * 1024 + 1024, :],
                (((1,), (1,)), ((), ())),
                preferred_element_type=F32,
            )
            o_ref[2 * k + q] = part.astype(BF16)
            cols = pl.ds(pl.multiple_of(blocks[k] * 2048 + q * 1024, 1024), 1024)
            out = pltpu.make_async_copy(o_ref.at[2 * k + q], update.at[:, cols], o_sem.at[2 * k + q])
            out.start()
            stores.append(out)
    for out in stores:
        out.wait()


def last_stage(at, mine, got, first, second, held, late):
    rows = first.shape[0]
    moment = jax.ShapeDtypeStruct((rows, 512), F32)
    args = [
        pltpu.with_memory_space_constraint(a, pltpu.VMEM)
        for a in (mine, got, first, second) + tuple(held)
    ]
    args += [pltpu.with_memory_space_constraint(a, pltpu.HBM) for a in late]
    return pl.pallas_call(
        last_kernel,
        in_specs=[SMEM] + [VMEM] * 6 + [HBM] * 2,
        out_specs=[HBM] * 3,
        out_shape=[moment, moment, jax.ShapeDtypeStruct((rows, 8192), BF16)],
        scratch_shapes=[
            pltpu.VMEM((2, 2048, 512), BF16),
            pltpu.VMEM((2, rows, 512), F32),
            pltpu.VMEM((8, rows, 1024), BF16),
            pltpu.SemaphoreType.DMA((4,)),
            pltpu.SemaphoreType.DMA((2,)),
            pltpu.SemaphoreType.DMA((8,)),
        ],
        compiler_params=params(12),
        name="last",
    )(at, *args)


def step(inputs, gate_preact, hidden_grad, projector, first_moment, second_moment):
    x, z, yl, yh, c = (lax.axis_index(a).astype(jnp.int32) for a in AXES)
    at = jnp.stack([x, z, c, yh])

    mine, theirs, *pieces = front(at, gate_preact, hidden_grad, inputs, projector)
    got_x = [pieces[0]] + [shift(pieces[k], "x", k) for k in (1, 2, 3)]
    got_z = [pieces[4]] + [shift(pieces[4 + k], "z", k) for k in (1, 2, 3)]

    chip_sum = mine + shift(theirs, "c", 1)
    far = shift(chip_sum.astype(BF16), "yh", 1)
    half = (chip_sum + far.astype(F32)).astype(BF16)
    own = join(at, half, shift(half, "c", 1))
    along = {k: cross(own, k) for k in (1, 3, 2)}
    beyond = {k: shift(along[k], "c", 1) for k in (1, 3, 2)}

    near_w = lax.ppermute(projector, ("yl", "yh"), [(0, 3), (3, 0), (1, 2), (2, 1)])
    beside_w = shift(projector, "c", 1)
    across_w = shift(near_w, "c", 1)

    parts = []
    for got, pick, axis in ((got_z, 1 - c, "x"), (got_x, c, "z")):
        near = (own, along[1], beyond[1], along[3], beyond[3])
        acc = early_sums(pick, (got[0], got[1], got[3]), near)
        part = late_sums(pick, acc, got[2], (along[2], beyond[2]))
        parts.append([part[0]] + [shift(part[k], axis, k) for k in (1, 2, 3)])
    parts_z, parts_x = parts
    keep, give = combine(yl, parts_x, parts_z)
    got = shift(give, "yl", 1)
    held = hold((projector, beside_w))
    return last_stage(at, keep, got, first_moment, second_moment, held, (near_w, across_w))


def solution(mesh):
    fine = Mesh(mesh.devices.reshape(4, 4, 2, 2, 2), ("x", "z", "yl", "yh", "c"))
    dp, mp = ("x", "z", "yl"), ("yh", "c")
    return jax.shard_map(
        step,
        mesh=fine,
        in_specs=(P(dp, mp), P(dp, mp), P(dp, mp), P(mp, None), P(mp + dp, None), P(mp + dp, None)),
        out_specs=(P(mp + dp, None),) * 3,
        check_vma=False,
    )
```

```python
import jax
import jax.numpy as jnp
from jax import lax
from jax.experimental import pallas as pl
from jax.experimental.pallas import tpu as pltpu
from jax.sharding import Mesh, PartitionSpec as P


F32 = jnp.float32
BF16 = jnp.bfloat16
SIZE = {"x": 4, "z": 4, "yl": 2, "yh": 2, "c": 2}
SMEM = pl.BlockSpec(memory_space=pltpu.SMEM)
VMEM = pl.BlockSpec(memory_space=pltpu.VMEM)
HBM = pl.BlockSpec(memory_space=pl.ANY)
AXES = ("x", "z", "yl", "yh", "c")


def params(mib):
    return pltpu.CompilerParams(vmem_limit_bytes=mib * 1024 * 1024)


def shift(a, axis, k):
    n = SIZE[axis]
    return lax.ppermute(a, axis, [(i, (i + k) % n) for i in range(n)])


def cross(a, first, k):
    pairs = []
    for i in range(128):
        x, z, rest = i // 32, i // 8 % 4, i % 8
        if (i % 2 == 0) == (first == "x"):
            x = (x + k) % 4
        else:
            z = (z + k) % 4
        pairs.append((i, x * 32 + z * 8 + rest))
    return lax.ppermute(a, AXES, pairs)


def front_kernel(s_ref, g_ref, h_ref, i_ref, w_ref, mine, theirs, *rest):
    outs, t_ref = rest[:-1], rest[-1]
    to_x, to_z = outs[:4], outs[4:]
    i = pl.program_id(0)
    for b in range(14):
        cols = slice(b * 128, b * 128 + 128)
        v = 0.5 * g_ref[:, cols].astype(F32)
        w = v * h_ref[:, cols].astype(F32)
        t_ref[cols, :] = (w + w * jnp.tanh(v)).astype(BF16).T
    c = s_ref[2]
    for out, half in ((mine, c), (theirs, 1 - c)):
        start = pl.multiple_of(half * 256, 256)
        part = jnp.dot(i_ref[...], w_ref[:, pl.ds(start, 256)], preferred_element_type=F32)

        @pl.when(i == 0)
        def _():
            out[...] = part

        @pl.when(i > 0)
        def _():
            out[...] += part

    for k in range(4):
        start = pl.multiple_of(lax.rem(s_ref[1] + k, 4) * 448, 448)
        to_z[k][i] = t_ref[pl.ds(start + 224, 224), :]
        for j in range(4):

            @pl.when(i == j)
            def _():
                to_x[j][k] = t_ref[pl.ds(start, 224), :]


def front(at, gate, hidden, inputs, projector):
    t = gate.shape[0]
    block = pl.BlockSpec((t, 1792), lambda i, s: (0, lax.rem(s[0] + i, 4)))
    args = [
        pltpu.with_memory_space_constraint(a, pltpu.HBM) for a in (gate, hidden, inputs, projector)
    ]
    return pl.pallas_call(
        front_kernel,
        grid_spec=pltpu.PrefetchScalarGridSpec(
            num_scalar_prefetch=1,
            grid=(4,),
            in_specs=[
                block,
                block,
                pl.BlockSpec((t, 512), lambda i, s: (0, i)),
                pl.BlockSpec((512, 512), lambda i, s: (i, 0)),
            ],
            out_specs=[VMEM] * 10,
            scratch_shapes=[pltpu.VMEM((1792, t), BF16)],
        ),
        out_shape=[pltpu.VMEM((t, 256), F32)] * 2 + [pltpu.VMEM((4, 224, t), BF16)] * 8,
        compiler_params=params(16),
        name="front",
    )(at, *args)


def join_kernel(s_ref, half, other, out):
    c = s_ref[2]
    out[:, pl.ds(pl.multiple_of(c * 256, 256), 256)] = half[...]
    out[:, pl.ds(pl.multiple_of(256 - c * 256, 256), 256)] = other[...]


def join(at, half, other):
    args = [pltpu.with_memory_space_constraint(a, pltpu.VMEM) for a in (half, other)]
    return pl.pallas_call(
        join_kernel,
        in_specs=[SMEM, VMEM, VMEM],
        out_specs=VMEM,
        out_shape=pltpu.VMEM((half.shape[0], 512), BF16),
        compiler_params=params(4),
        name="join",
    )(at, *args)


def hold_kernel(a, b, x, y, sem):
    copies = []
    for k, (src, dst) in enumerate(((a, x), (b, y))):
        for q in range(2):
            rows = pl.ds(q * 1024, 1024)
            copies.append(pltpu.make_async_copy(src.at[rows], dst.at[rows], sem.at[2 * k + q]))
    for copy in copies:
        copy.start()
    for copy in copies:
        copy.wait()


def hold(blocks):
    args = [pltpu.with_memory_space_constraint(a, pltpu.HBM) for a in blocks]
    return pl.pallas_call(
        hold_kernel,
        in_specs=[HBM] * 2,
        out_specs=[VMEM] * 2,
        out_shape=[pltpu.VMEM((2048, 512), BF16)] * 2,
        scratch_shapes=[pltpu.SemaphoreType.DMA((4,))],
        compiler_params=params(1),
        name="keep",
    )(*args)


def load(use_x, piece_x, piece_z, dst, sem):
    for use, src in ((1, piece_x), (0, piece_z)):

        @pl.when(use_x == use)
        def _():
            pltpu.make_async_copy(src, dst, sem).start()

    return pltpu.make_async_copy(piece_x, dst, sem)


def early_kernel(s_ref, x0, x1, x3, z0, z1, z3, c0, c1, c3, out, lhs, rhs, sem):
    pairs = ((x0, z0), (x1, z1), (x3, z3))
    loads = [
        [
            load(s_ref[0], a.at[j], b.at[j], lhs.at[j, :, pl.ds(n * 384, 384)], sem.at[j, n])
            for n, (a, b) in enumerate(pairs)
        ]
        for j in range(4)
    ]
    for n, coords in enumerate((c0, c1, c3)):
        rhs[n * 384 : n * 384 + 384, :] = coords[...]
    for j in range(4):
        for copy in loads[j]:
            copy.wait()
        out[j] = jnp.dot(lhs[j], rhs[...], preferred_element_type=F32)


def early_sums(use_x, pieces, coords):
    t = pieces[0].shape[-1]
    args = [pltpu.with_memory_space_constraint(a, pltpu.HBM) for a in pieces]
    args += [pltpu.with_memory_space_constraint(a, pltpu.VMEM) for a in coords]
    return pl.pallas_call(
        early_kernel,
        in_specs=[SMEM] + [HBM] * 6 + [VMEM] * 3,
        out_specs=VMEM,
        out_shape=pltpu.VMEM((4, 224, 512), F32),
        scratch_shapes=[
            pltpu.VMEM((4, 224, 3 * t), BF16),
            pltpu.VMEM((3 * t, 512), BF16),
            pltpu.SemaphoreType.DMA((4, 3)),
        ],
        compiler_params=params(8),
    )(use_x.reshape(1), *args)


def late_kernel(s_ref, acc, coords, x2, z2, o0, o1, o2, o3, lhs, sem):
    order = (1, 3, 2, 0)
    loads = {j: load(s_ref[0], x2.at[j], z2.at[j], lhs.at[j], sem.at[j]) for j in order}
    for j in order:
        out = (o0, o1, o2, o3)[j]
        loads[j].wait()
        part = acc[j] + jnp.dot(lhs[j], coords[...], preferred_element_type=F32)
        out[...] = part.astype(out.dtype)


def late_sums(use_x, acc, coords, pieces):
    t = pieces[0].shape[-1]
    args = [pltpu.with_memory_space_constraint(a, pltpu.VMEM) for a in (acc, coords)]
    args += [pltpu.with_memory_space_constraint(a, pltpu.HBM) for a in pieces]
    return pl.pallas_call(
        late_kernel,
        in_specs=[SMEM] + [VMEM] * 2 + [HBM] * 2,
        out_specs=[VMEM] * 4,
        out_shape=[pltpu.VMEM((224, 512), F32)] + [pltpu.VMEM((224, 512), BF16)] * 3,
        scratch_shapes=[pltpu.VMEM((4, 224, t), BF16), pltpu.SemaphoreType.DMA((4,))],
        compiler_params=params(6),
    )(use_x.reshape(1), *args)


def combine_kernel(s_ref, m0, m1, m2, m3, t0, t1, t2, t3, keep, give):
    mine = m0[...] + m1[...].astype(F32) + m2[...].astype(F32) + m3[...].astype(F32)
    theirs = t0[...] + t1[...].astype(F32) + t2[...].astype(F32) + t3[...].astype(F32)
    here = s_ref[0] == 1
    keep[...] = jnp.where(here, mine, theirs)
    give[...] = jnp.where(here, theirs, mine).astype(BF16)


def combine(keep_mine, mine, theirs):
    args = [pltpu.with_memory_space_constraint(a, pltpu.VMEM) for a in (*mine, *theirs)]
    return pl.pallas_call(
        combine_kernel,
        in_specs=[SMEM] + [VMEM] * 8,
        out_specs=[VMEM] * 2,
        out_shape=[pltpu.VMEM((224, 512), F32), pltpu.VMEM((224, 512), BF16)],
        compiler_params=params(4),
        name="combine",
    )(keep_mine.reshape(1), *args)


def last_kernel(
    s_ref, mine, got, first, second, w0, w1, w2, w3, new_first, new_second, update,
    w_ref, m_ref, o_ref, w_sem, m_sem, o_sem,
):
    yh, c = s_ref[3], s_ref[2]
    loads = []
    for q in range(2):
        rows = pl.ds(q * 1024, 1024)
        loads.append(pltpu.make_async_copy(w3.at[rows], w_ref.at[rows], w_sem.at[q]))
        loads[q].start()
    projected = mine[...] + got[...].astype(F32)
    m = 0.9 * first[...] + 0.1 * projected
    v = 0.95 * second[...] + 0.05 * projected * projected
    m_ref[0] = m
    m_ref[1] = v
    stores = [
        pltpu.make_async_copy(m_ref.at[k], out, m_sem.at[k])
        for k, out in enumerate((new_first, new_second))
    ]
    for out in stores:
        out.start()
    root = jnp.sqrt(v * (1.0 / (1.0 - 0.9025)))
    direction = (m * (1.0 / (1.0 - 0.81)) / (root + 1e-08)).astype(BF16)
    blocks = (2 * yh + c, 2 * yh + 1 - c, 3 - 2 * yh - c, 2 - 2 * yh + c)
    for k, w in enumerate((w0, w1, w2, w_ref)):
        for q in range(2):
            if k == 3:
                loads[q].wait()
            part = 4.0 * lax.dot_general(
                direction,
                w[q * 1024 : q * 1024 + 1024, :],
                (((1,), (1,)), ((), ())),
                preferred_element_type=F32,
            )
            o_ref[2 * k + q] = part.astype(BF16)
            cols = pl.ds(pl.multiple_of(blocks[k] * 2048 + q * 1024, 1024), 1024)
            out = pltpu.make_async_copy(o_ref.at[2 * k + q], update.at[:, cols], o_sem.at[2 * k + q])
            out.start()
            stores.append(out)
    for out in stores:
        out.wait()


def last_stage(at, mine, got, first, second, blocks, near):
    rows = first.shape[0]
    moment = jax.ShapeDtypeStruct((rows, 512), F32)
    args = [
        pltpu.with_memory_space_constraint(a, pltpu.VMEM)
        for a in (mine, got, first, second) + tuple(blocks)
    ]
    args.append(pltpu.with_memory_space_constraint(near, pltpu.HBM))
    return pl.pallas_call(
        last_kernel,
        in_specs=[SMEM] + [VMEM] * 7 + [HBM],
        out_specs=[HBM] * 3,
        out_shape=[moment, moment, jax.ShapeDtypeStruct((rows, 8192), BF16)],
        scratch_shapes=[
            pltpu.VMEM((2048, 512), BF16),
            pltpu.VMEM((2, rows, 512), F32),
            pltpu.VMEM((8, rows, 1024), BF16),
            pltpu.SemaphoreType.DMA((2,)),
            pltpu.SemaphoreType.DMA((2,)),
            pltpu.SemaphoreType.DMA((8,)),
        ],
        compiler_params=params(12),
        name="last",
    )(at, *args)


def step(inputs, gate_preact, hidden_grad, projector, first_moment, second_moment):
    x, z, yl, yh, c = (lax.axis_index(a).astype(jnp.int32) for a in AXES)
    at = jnp.stack([x, z, c, yh])

    mine, theirs, *pieces = front(at, gate_preact, hidden_grad, inputs, projector)
    got_x = [pieces[0]] + [shift(pieces[k], "x", k) for k in (1, 2, 3)]
    got_z = [pieces[4]] + [shift(pieces[4 + k], "z", k) for k in (1, 2, 3)]

    chip_sum = mine + shift(theirs, "c", 1)
    far = shift(chip_sum.astype(BF16), "yh", 1)
    half = (chip_sum + far.astype(F32)).astype(BF16)
    own = join(at, half, shift(half, "c", 1))
    along = {k: cross(own, "x", k) for k in (1, 3, 2)}
    beyond = {k: shift(along[k], "c", 1) for k in (1, 3, 2)}

    near_w = lax.ppermute(projector, ("yl", "yh"), [(0, 3), (3, 0), (1, 2), (2, 1)])
    beside_w = shift(projector, "c", 1)
    across_w = shift(near_w, "c", 1)

    near = [got[k] for got in (got_x, got_z) for k in (0, 1, 3)]
    sums = []
    for use_x, coords, axis in ((1 - c, along, "z"), (c, beyond, "x")):
        acc = early_sums(use_x, near, (own, coords[1], coords[3]))
        part = late_sums(use_x, acc, coords[2], (got_x[2], got_z[2]))
        sums.append([part[0]] + [cross(part[k], axis, k) for k in (1, 2, 3)])
    keep, give = combine(1 - jnp.bitwise_xor(c, yl), *sums)
    got = shift(give, "yl", 1)
    held = hold((projector, beside_w))
    return last_stage(at, keep, got, first_moment, second_moment, (*held, across_w), near_w)


def solution(mesh):
    fine = Mesh(mesh.devices.reshape(4, 4, 2, 2, 2), ("x", "z", "yl", "yh", "c"))
    dp, mp = ("x", "z", "yl"), ("yh", "c")
    return jax.shard_map(
        step,
        mesh=fine,
        in_specs=(P(dp, mp), P(dp, mp), P(dp, mp), P(mp, None), P(mp + dp, None), P(mp + dp, None)),
        out_specs=(P(mp + dp, None),) * 3,
        check_vma=False,
    )
```

```python
import jax
import jax.numpy as jnp
from jax import lax
from jax.experimental import pallas as pl
from jax.experimental.pallas import tpu as pltpu
from jax.sharding import Mesh, PartitionSpec as P


F32 = jnp.float32
BF16 = jnp.bfloat16
SIZE = {"x": 4, "z": 4, "yl": 2, "yh": 2, "c": 2}
SMEM = pl.BlockSpec(memory_space=pltpu.SMEM)
VMEM = pl.BlockSpec(memory_space=pltpu.VMEM)
HBM = pl.BlockSpec(memory_space=pl.ANY)
AXES = ("x", "z", "yl", "yh", "c")


def params(mib):
    return pltpu.CompilerParams(vmem_limit_bytes=mib * 1024 * 1024)


def shift(a, axis, k):
    n = SIZE[axis]
    return lax.ppermute(a, axis, [(i, (i + k) % n) for i in range(n)])


def cross(a, first, k):
    pairs = []
    for i in range(128):
        x, z, rest = i // 32, i // 8 % 4, i % 8
        if (i % 2 == 0) == (first == "x"):
            x = (x + k) % 4
        else:
            z = (z + k) % 4
        pairs.append((i, x * 32 + z * 8 + rest))
    return lax.ppermute(a, AXES, pairs)


def front_kernel(s_ref, g_ref, h_ref, i_ref, w_ref, mine, theirs, *rest):
    outs, t_ref = rest[:-1], rest[-1]
    to_x, to_z = outs[:4], outs[4:]
    i = pl.program_id(0)
    for b in range(14):
        cols = slice(b * 128, b * 128 + 128)
        v = 0.5 * g_ref[:, cols].astype(F32)
        w = v * h_ref[:, cols].astype(F32)
        t_ref[cols, :] = (w + w * jnp.tanh(v)).astype(BF16).T
    c = s_ref[2]
    for out, half in ((mine, c), (theirs, 1 - c)):
        start = pl.multiple_of(half * 256, 256)
        part = jnp.dot(i_ref[...], w_ref[:, pl.ds(start, 256)], preferred_element_type=F32)

        @pl.when(i == 0)
        def _():
            out[...] = part

        @pl.when(i > 0)
        def _():
            out[...] += part

    for k in range(4):
        start = pl.multiple_of(lax.rem(s_ref[1] + k, 4) * 448, 448)
        to_z[k][i] = t_ref[pl.ds(start + 224, 224), :]
        for j in range(4):

            @pl.when(i == j)
            def _():
                to_x[j][k] = t_ref[pl.ds(start, 224), :]


def front(at, gate, hidden, inputs, projector):
    t = gate.shape[0]
    block = pl.BlockSpec((t, 1792), lambda i, s: (0, lax.rem(s[0] + i, 4)))
    args = [
        pltpu.with_memory_space_constraint(a, pltpu.HBM) for a in (gate, hidden, inputs, projector)
    ]
    return pl.pallas_call(
        front_kernel,
        grid_spec=pltpu.PrefetchScalarGridSpec(
            num_scalar_prefetch=1,
            grid=(4,),
            in_specs=[
                block,
                block,
                pl.BlockSpec((t, 512), lambda i, s: (0, i)),
                pl.BlockSpec((512, 512), lambda i, s: (i, 0)),
            ],
            out_specs=[VMEM] * 10,
            scratch_shapes=[pltpu.VMEM((1792, t), BF16)],
        ),
        out_shape=[pltpu.VMEM((t, 256), F32)] * 2 + [pltpu.VMEM((4, 224, t), BF16)] * 8,
        compiler_params=params(16),
        name="front",
    )(at, *args)


def join_kernel(s_ref, half, other, out):
    c = s_ref[2]
    out[:, pl.ds(pl.multiple_of(c * 256, 256), 256)] = half[...]
    out[:, pl.ds(pl.multiple_of(256 - c * 256, 256), 256)] = other[...]


def join(at, half, other):
    args = [pltpu.with_memory_space_constraint(a, pltpu.VMEM) for a in (half, other)]
    return pl.pallas_call(
        join_kernel,
        in_specs=[SMEM, VMEM, VMEM],
        out_specs=VMEM,
        out_shape=pltpu.VMEM((half.shape[0], 512), BF16),
        compiler_params=params(4),
        name="join",
    )(at, *args)


def hold_kernel(a, b, x, y, sem):
    copies = []
    for k, (src, dst) in enumerate(((a, x), (b, y))):
        for q in range(2):
            rows = pl.ds(q * 1024, 1024)
            copies.append(pltpu.make_async_copy(src.at[rows], dst.at[rows], sem.at[2 * k + q]))
    for copy in copies:
        copy.start()
    for copy in copies:
        copy.wait()


def hold(blocks):
    args = [pltpu.with_memory_space_constraint(a, pltpu.HBM) for a in blocks]
    return pl.pallas_call(
        hold_kernel,
        in_specs=[HBM] * 2,
        out_specs=[VMEM] * 2,
        out_shape=[pltpu.VMEM((2048, 512), BF16)] * 2,
        scratch_shapes=[pltpu.SemaphoreType.DMA((4,))],
        compiler_params=params(1),
        name="keep",
    )(*args)


def load(use_x, piece_x, piece_z, dst, sem):
    for use, src in ((1, piece_x), (0, piece_z)):

        @pl.when(use_x == use)
        def _():
            pltpu.make_async_copy(src, dst, sem).start()

    return pltpu.make_async_copy(piece_x, dst, sem)


def early_kernel(s_ref, x0, x1, x3, z0, z1, z3, c0, c1, c3, out, lhs, rhs, sem):
    pairs = ((x0, z0), (x1, z1), (x3, z3))
    loads = [
        [
            load(s_ref[0], a.at[j], b.at[j], lhs.at[j, :, pl.ds(n * 384, 384)], sem.at[j, n])
            for n, (a, b) in enumerate(pairs)
        ]
        for j in range(4)
    ]
    for n, coords in enumerate((c0, c1, c3)):
        rhs[n * 384 : n * 384 + 384, :] = coords[...]
    for j in range(4):
        for copy in loads[j]:
            copy.wait()
        out[j] = jnp.dot(lhs[j], rhs[...], preferred_element_type=F32)


def early_sums(use_x, pieces, coords):
    t = pieces[0].shape[-1]
    args = [pltpu.with_memory_space_constraint(a, pltpu.HBM) for a in pieces]
    args += [pltpu.with_memory_space_constraint(a, pltpu.VMEM) for a in coords]
    return pl.pallas_call(
        early_kernel,
        in_specs=[SMEM] + [HBM] * 6 + [VMEM] * 3,
        out_specs=VMEM,
        out_shape=pltpu.VMEM((4, 224, 512), F32),
        scratch_shapes=[
            pltpu.VMEM((4, 224, 3 * t), BF16),
            pltpu.VMEM((3 * t, 512), BF16),
            pltpu.SemaphoreType.DMA((4, 3)),
        ],
        compiler_params=params(8),
    )(use_x.reshape(1), *args)


def late_kernel(s_ref, acc, coords, x2, z2, o0, o1, o2, o3):
    for use, piece in ((1, x2), (0, z2)):

        @pl.when(s_ref[0] == use)
        def _():
            for j, out in enumerate((o0, o1, o2, o3)):
                part = acc[j] + jnp.dot(piece[j], coords[...], preferred_element_type=F32)
                out[...] = part.astype(out.dtype)


def late_sums(use_x, acc, coords, pieces):
    args = [pltpu.with_memory_space_constraint(a, pltpu.VMEM) for a in (acc, coords, *pieces)]
    return pl.pallas_call(
        late_kernel,
        in_specs=[SMEM] + [VMEM] * 4,
        out_specs=[VMEM] * 4,
        out_shape=[pltpu.VMEM((224, 512), F32)] + [pltpu.VMEM((224, 512), BF16)] * 3,
        compiler_params=params(4),
    )(use_x.reshape(1), *args)


def combine_kernel(s_ref, m0, m1, m2, m3, t0, t1, t2, t3, keep, give):
    mine = m0[...] + m1[...].astype(F32) + m2[...].astype(F32) + m3[...].astype(F32)
    theirs = t0[...] + t1[...].astype(F32) + t2[...].astype(F32) + t3[...].astype(F32)
    here = s_ref[0] == 1
    keep[...] = jnp.where(here, mine, theirs)
    give[...] = jnp.where(here, theirs, mine).astype(BF16)


def combine(keep_mine, mine, theirs):
    args = [pltpu.with_memory_space_constraint(a, pltpu.VMEM) for a in (*mine, *theirs)]
    return pl.pallas_call(
        combine_kernel,
        in_specs=[SMEM] + [VMEM] * 8,
        out_specs=[VMEM] * 2,
        out_shape=[pltpu.VMEM((224, 512), F32), pltpu.VMEM((224, 512), BF16)],
        compiler_params=params(4),
        name="combine",
    )(keep_mine.reshape(1), *args)


def last_kernel(
    s_ref, mine, got, first, second, w0, w1, w2, w3, new_first, new_second, update,
    w_ref, m_ref, o_ref, w_sem, m_sem, o_sem,
):
    yh, c = s_ref[3], s_ref[2]
    loads = []
    for q in range(2):
        rows = pl.ds(q * 1024, 1024)
        loads.append(pltpu.make_async_copy(w3.at[rows], w_ref.at[rows], w_sem.at[q]))
        loads[q].start()
    projected = mine[...] + got[...].astype(F32)
    m = 0.9 * first[...] + 0.1 * projected
    v = 0.95 * second[...] + 0.05 * projected * projected
    m_ref[0] = m
    m_ref[1] = v
    stores = [
        pltpu.make_async_copy(m_ref.at[k], out, m_sem.at[k])
        for k, out in enumerate((new_first, new_second))
    ]
    for out in stores:
        out.start()
    root = jnp.sqrt(v * (1.0 / (1.0 - 0.9025)))
    direction = (m * (1.0 / (1.0 - 0.81)) / (root + 1e-08)).astype(BF16)
    blocks = (2 * yh + c, 2 * yh + 1 - c, 3 - 2 * yh - c, 2 - 2 * yh + c)
    for k, w in enumerate((w0, w1, w2, w_ref)):
        for q in range(2):
            if k == 3:
                loads[q].wait()
            part = 4.0 * lax.dot_general(
                direction,
                w[q * 1024 : q * 1024 + 1024, :],
                (((1,), (1,)), ((), ())),
                preferred_element_type=F32,
            )
            o_ref[2 * k + q] = part.astype(BF16)
            cols = pl.ds(pl.multiple_of(blocks[k] * 2048 + q * 1024, 1024), 1024)
            out = pltpu.make_async_copy(o_ref.at[2 * k + q], update.at[:, cols], o_sem.at[2 * k + q])
            out.start()
            stores.append(out)
    for out in stores:
        out.wait()


def last_stage(at, mine, got, first, second, blocks, near):
    rows = first.shape[0]
    moment = jax.ShapeDtypeStruct((rows, 512), F32)
    args = [
        pltpu.with_memory_space_constraint(a, pltpu.VMEM)
        for a in (mine, got, first, second) + tuple(blocks)
    ]
    args.append(pltpu.with_memory_space_constraint(near, pltpu.HBM))
    return pl.pallas_call(
        last_kernel,
        in_specs=[SMEM] + [VMEM] * 7 + [HBM],
        out_specs=[HBM] * 3,
        out_shape=[moment, moment, jax.ShapeDtypeStruct((rows, 8192), BF16)],
        scratch_shapes=[
            pltpu.VMEM((2048, 512), BF16),
            pltpu.VMEM((2, rows, 512), F32),
            pltpu.VMEM((8, rows, 1024), BF16),
            pltpu.SemaphoreType.DMA((2,)),
            pltpu.SemaphoreType.DMA((2,)),
            pltpu.SemaphoreType.DMA((8,)),
        ],
        compiler_params=params(12),
        name="last",
    )(at, *args)


def step(inputs, gate_preact, hidden_grad, projector, first_moment, second_moment):
    x, z, yl, yh, c = (lax.axis_index(a).astype(jnp.int32) for a in AXES)
    at = jnp.stack([x, z, c, yh])

    mine, theirs, *pieces = front(at, gate_preact, hidden_grad, inputs, projector)
    got_x = [pieces[0]] + [shift(pieces[k], "x", k) for k in (1, 2, 3)]
    got_z = [pieces[4]] + [shift(pieces[4 + k], "z", k) for k in (1, 2, 3)]

    chip_sum = mine + shift(theirs, "c", 1)
    far = shift(chip_sum.astype(BF16), "yh", 1)
    half = (chip_sum + far.astype(F32)).astype(BF16)
    own = join(at, half, shift(half, "c", 1))
    along = {k: cross(own, "x", k) for k in (1, 3, 2)}
    beyond = {k: shift(along[k], "c", 1) for k in (1, 3, 2)}

    near_w = lax.ppermute(projector, ("yl", "yh"), [(0, 3), (3, 0), (1, 2), (2, 1)])
    beside_w = shift(projector, "c", 1)
    across_w = shift(near_w, "c", 1)

    near = [got[k] for got in (got_x, got_z) for k in (0, 1, 3)]
    sums = []
    for use_x, coords, axis in ((1 - c, along, "z"), (c, beyond, "x")):
        acc = early_sums(use_x, near, (own, coords[1], coords[3]))
        part = late_sums(use_x, acc, coords[2], (got_x[2], got_z[2]))
        sums.append([part[0]] + [cross(part[k], axis, k) for k in (1, 2, 3)])
    keep, give = combine(1 - jnp.bitwise_xor(c, yl), *sums)
    got = shift(give, "yl", 1)
    held = hold((projector, beside_w))
    return last_stage(at, keep, got, first_moment, second_moment, (*held, across_w), near_w)


def solution(mesh):
    fine = Mesh(mesh.devices.reshape(4, 4, 2, 2, 2), ("x", "z", "yl", "yh", "c"))
    dp, mp = ("x", "z", "yl"), ("yh", "c")
    return jax.shard_map(
        step,
        mesh=fine,
        in_specs=(P(dp, mp), P(dp, mp), P(dp, mp), P(mp, None), P(mp + dp, None), P(mp + dp, None)),
        out_specs=(P(mp + dp, None),) * 3,
        check_vma=False,
    )
```

```python
import jax
import jax.numpy as jnp
from jax import lax
from jax.experimental import pallas as pl
from jax.experimental.pallas import tpu as pltpu
from jax.sharding import Mesh, PartitionSpec as P


F32 = jnp.float32
BF16 = jnp.bfloat16
SIZE = {"x": 4, "z": 4, "yl": 2, "yh": 2, "c": 2}
SMEM = pl.BlockSpec(memory_space=pltpu.SMEM)
VMEM = pl.BlockSpec(memory_space=pltpu.VMEM)
HBM = pl.BlockSpec(memory_space=pl.ANY)
AXES = ("x", "z", "yl", "yh", "c")


def params(mib):
    return pltpu.CompilerParams(vmem_limit_bytes=mib * 1024 * 1024)


def shift(a, axis, k):
    n = SIZE[axis]
    return lax.ppermute(a, axis, [(i, (i + k) % n) for i in range(n)])


def cross(a, first, k):
    pairs = []
    for i in range(128):
        x, z, rest = i // 32, i // 8 % 4, i % 8
        if (i % 2 == 0) == (first == "x"):
            x = (x + k) % 4
        else:
            z = (z + k) % 4
        pairs.append((i, x * 32 + z * 8 + rest))
    return lax.ppermute(a, AXES, pairs)


def front_kernel(s_ref, g_ref, h_ref, i_ref, w_ref, mine, theirs, *rest):
    outs, t_ref = rest[:-1], rest[-1]
    to_x, to_z = outs[:4], outs[4:]
    i = pl.program_id(0)
    for b in range(14):
        cols = slice(b * 128, b * 128 + 128)
        v = 0.5 * g_ref[:, cols].astype(F32)
        w = v * h_ref[:, cols].astype(F32)
        t_ref[cols, :] = (w + w * jnp.tanh(v)).astype(BF16).T
    c = s_ref[2]
    for out, half in ((mine, c), (theirs, 1 - c)):
        start = pl.multiple_of(half * 256, 256)
        part = jnp.dot(i_ref[...], w_ref[:, pl.ds(start, 256)], preferred_element_type=F32)

        @pl.when(i == 0)
        def _():
            out[...] = part

        @pl.when(i > 0)
        def _():
            out[...] += part

    for k in range(4):
        start = pl.multiple_of(lax.rem(s_ref[1] + k, 4) * 448, 448)
        to_z[k][i] = t_ref[pl.ds(start + 224, 224), :]
        for j in range(4):

            @pl.when(i == j)
            def _():
                to_x[j][k] = t_ref[pl.ds(start, 224), :]


def front(at, gate, hidden, inputs, projector):
    t = gate.shape[0]
    block = pl.BlockSpec((t, 1792), lambda i, s: (0, lax.rem(s[0] + i, 4)))
    args = [
        pltpu.with_memory_space_constraint(a, pltpu.HBM) for a in (gate, hidden, inputs, projector)
    ]
    return pl.pallas_call(
        front_kernel,
        grid_spec=pltpu.PrefetchScalarGridSpec(
            num_scalar_prefetch=1,
            grid=(4,),
            in_specs=[
                block,
                block,
                pl.BlockSpec((t, 512), lambda i, s: (0, i)),
                pl.BlockSpec((512, 512), lambda i, s: (i, 0)),
            ],
            out_specs=[VMEM] * 10,
            scratch_shapes=[pltpu.VMEM((1792, t), BF16)],
        ),
        out_shape=[pltpu.VMEM((t, 256), F32)] * 2 + [pltpu.VMEM((4, 224, t), BF16)] * 8,
        compiler_params=params(16),
        name="front",
    )(at, *args)


def join_kernel(s_ref, half, other, out):
    c = s_ref[2]
    out[:, pl.ds(pl.multiple_of(c * 256, 256), 256)] = half[...]
    out[:, pl.ds(pl.multiple_of(256 - c * 256, 256), 256)] = other[...]


def join(at, half, other):
    args = [pltpu.with_memory_space_constraint(a, pltpu.VMEM) for a in (half, other)]
    return pl.pallas_call(
        join_kernel,
        in_specs=[SMEM, VMEM, VMEM],
        out_specs=VMEM,
        out_shape=pltpu.VMEM((half.shape[0], 512), BF16),
        compiler_params=params(4),
        name="join",
    )(at, *args)


def hold_kernel(a, b, x, y, sem):
    copies = []
    for k, (src, dst) in enumerate(((a, x), (b, y))):
        for q in range(2):
            rows = pl.ds(q * 1024, 1024)
            copies.append(pltpu.make_async_copy(src.at[rows], dst.at[rows], sem.at[2 * k + q]))
    for copy in copies:
        copy.start()
    for copy in copies:
        copy.wait()


def hold(blocks):
    args = [pltpu.with_memory_space_constraint(a, pltpu.HBM) for a in blocks]
    return pl.pallas_call(
        hold_kernel,
        in_specs=[HBM] * 2,
        out_specs=[VMEM] * 2,
        out_shape=[pltpu.VMEM((2048, 512), BF16)] * 2,
        scratch_shapes=[pltpu.SemaphoreType.DMA((4,))],
        compiler_params=params(1),
        name="keep",
    )(*args)


def load(use_x, piece_x, piece_z, dst, sem):
    for use, src in ((1, piece_x), (0, piece_z)):

        @pl.when(use_x == use)
        def _():
            pltpu.make_async_copy(src, dst, sem).start()

    return pltpu.make_async_copy(piece_x, dst, sem)


def early_kernel(s_ref, x0, x2, z0, z2, c0, c2, out, lhs, rhs, sem):
    loads = [
        [
            load(s_ref[0], a.at[j], b.at[j], lhs.at[j, :, pl.ds(n * 384, 384)], sem.at[j, n])
            for n, (a, b) in enumerate(((x0, z0), (x2, z2)))
        ]
        for j in range(4)
    ]
    for n, coords in enumerate((c0, c2)):
        rhs[n * 384 : n * 384 + 384, :] = coords[...]
    for j in range(4):
        for copy in loads[j]:
            copy.wait()
        out[j] = jnp.dot(lhs[j], rhs[...], preferred_element_type=F32)


def early_sums(use_x, pieces, coords):
    t = pieces[0].shape[-1]
    args = [pltpu.with_memory_space_constraint(a, pltpu.HBM) for a in pieces]
    args += [pltpu.with_memory_space_constraint(a, pltpu.VMEM) for a in coords]
    return pl.pallas_call(
        early_kernel,
        in_specs=[SMEM] + [HBM] * 4 + [VMEM] * 2,
        out_specs=VMEM,
        out_shape=pltpu.VMEM((4, 224, 512), F32),
        scratch_shapes=[
            pltpu.VMEM((4, 224, 2 * t), BF16),
            pltpu.VMEM((2 * t, 512), BF16),
            pltpu.SemaphoreType.DMA((4, 2)),
        ],
        compiler_params=params(8),
    )(use_x.reshape(1), *args)


def late_kernel(s_ref, acc, c1, c3, x1, x3, z1, z3, o0, o1, o2, o3):
    for use, ones, threes in ((1, x1, x3), (0, z1, z3)):

        @pl.when(s_ref[0] == use)
        def _():
            for j, out in enumerate((o0, o1, o2, o3)):
                part = acc[j] + jnp.dot(ones[j], c1[...], preferred_element_type=F32)
                part += jnp.dot(threes[j], c3[...], preferred_element_type=F32)
                out[...] = part.astype(out.dtype)


def late_sums(use_x, acc, coords, pieces):
    args = [pltpu.with_memory_space_constraint(a, pltpu.VMEM) for a in (acc, *coords, *pieces)]
    return pl.pallas_call(
        late_kernel,
        in_specs=[SMEM] + [VMEM] * 7,
        out_specs=[VMEM] * 4,
        out_shape=[pltpu.VMEM((224, 512), F32)] + [pltpu.VMEM((224, 512), BF16)] * 3,
        compiler_params=params(6),
    )(use_x.reshape(1), *args)


def combine_kernel(s_ref, m0, m1, m2, m3, t0, t1, t2, t3, keep, give):
    mine = m0[...] + m1[...].astype(F32) + m2[...].astype(F32) + m3[...].astype(F32)
    theirs = t0[...] + t1[...].astype(F32) + t2[...].astype(F32) + t3[...].astype(F32)
    here = s_ref[0] == 1
    keep[...] = jnp.where(here, mine, theirs)
    give[...] = jnp.where(here, theirs, mine).astype(BF16)


def combine(keep_mine, mine, theirs):
    args = [pltpu.with_memory_space_constraint(a, pltpu.VMEM) for a in (*mine, *theirs)]
    return pl.pallas_call(
        combine_kernel,
        in_specs=[SMEM] + [VMEM] * 8,
        out_specs=[VMEM] * 2,
        out_shape=[pltpu.VMEM((224, 512), F32), pltpu.VMEM((224, 512), BF16)],
        compiler_params=params(4),
        name="combine",
    )(keep_mine.reshape(1), *args)


def last_kernel(
    s_ref, mine, got, first, second, w0, w1, w2, w3, new_first, new_second, update,
    w_ref, m_ref, o_ref, w_sem, m_sem, o_sem,
):
    yh, c = s_ref[3], s_ref[2]
    loads = []
    for q in range(2):
        rows = pl.ds(q * 1024, 1024)
        loads.append(pltpu.make_async_copy(w3.at[rows], w_ref.at[rows], w_sem.at[q]))
        loads[q].start()
    projected = mine[...] + got[...].astype(F32)
    m = 0.9 * first[...] + 0.1 * projected
    v = 0.95 * second[...] + 0.05 * projected * projected
    m_ref[0] = m
    m_ref[1] = v
    stores = [
        pltpu.make_async_copy(m_ref.at[k], out, m_sem.at[k])
        for k, out in enumerate((new_first, new_second))
    ]
    for out in stores:
        out.start()
    root = jnp.sqrt(v * (1.0 / (1.0 - 0.9025)))
    direction = (m * (1.0 / (1.0 - 0.81)) / (root + 1e-08)).astype(BF16)
    blocks = (2 * yh + c, 2 * yh + 1 - c, 3 - 2 * yh - c, 2 - 2 * yh + c)
    for k, w in enumerate((w0, w1, w2, w_ref)):
        for q in range(2):
            if k == 3:
                loads[q].wait()
            part = 4.0 * lax.dot_general(
                direction,
                w[q * 1024 : q * 1024 + 1024, :],
                (((1,), (1,)), ((), ())),
                preferred_element_type=F32,
            )
            o_ref[2 * k + q] = part.astype(BF16)
            cols = pl.ds(pl.multiple_of(blocks[k] * 2048 + q * 1024, 1024), 1024)
            out = pltpu.make_async_copy(o_ref.at[2 * k + q], update.at[:, cols], o_sem.at[2 * k + q])
            out.start()
            stores.append(out)
    for out in stores:
        out.wait()


def last_stage(at, mine, got, first, second, blocks, near):
    rows = first.shape[0]
    moment = jax.ShapeDtypeStruct((rows, 512), F32)
    args = [
        pltpu.with_memory_space_constraint(a, pltpu.VMEM)
        for a in (mine, got, first, second) + tuple(blocks)
    ]
    args.append(pltpu.with_memory_space_constraint(near, pltpu.HBM))
    return pl.pallas_call(
        last_kernel,
        in_specs=[SMEM] + [VMEM] * 7 + [HBM],
        out_specs=[HBM] * 3,
        out_shape=[moment, moment, jax.ShapeDtypeStruct((rows, 8192), BF16)],
        scratch_shapes=[
            pltpu.VMEM((2048, 512), BF16),
            pltpu.VMEM((2, rows, 512), F32),
            pltpu.VMEM((8, rows, 1024), BF16),
            pltpu.SemaphoreType.DMA((2,)),
            pltpu.SemaphoreType.DMA((2,)),
            pltpu.SemaphoreType.DMA((8,)),
        ],
        compiler_params=params(12),
        name="last",
    )(at, *args)


def step(inputs, gate_preact, hidden_grad, projector, first_moment, second_moment):
    x, z, yl, yh, c = (lax.axis_index(a).astype(jnp.int32) for a in AXES)
    at = jnp.stack([x, z, c, yh])

    mine, theirs, *pieces = front(at, gate_preact, hidden_grad, inputs, projector)
    got_x = [pieces[0]] + [shift(pieces[k], "x", k) for k in (1, 2, 3)]
    got_z = [pieces[4]] + [shift(pieces[4 + k], "z", k) for k in (1, 2, 3)]

    chip_sum = mine + shift(theirs, "c", 1)
    far = shift(chip_sum.astype(BF16), "yh", 1)
    half = (chip_sum + far.astype(F32)).astype(BF16)
    own = join(at, half, shift(half, "c", 1))
    along = {k: cross(own, "x", k) for k in (1, 3, 2)}
    beyond = {k: shift(along[k], "c", 1) for k in (1, 3, 2)}

    near_w = lax.ppermute(projector, ("yl", "yh"), [(0, 3), (3, 0), (1, 2), (2, 1)])
    beside_w = shift(projector, "c", 1)
    across_w = shift(near_w, "c", 1)

    first = [got[k] for got in (got_x, got_z) for k in (0, 2)]
    then = [got[k] for got in (got_x, got_z) for k in (1, 3)]
    sums = []
    for use_x, coords, axis in ((1 - c, along, "z"), (c, beyond, "x")):
        acc = early_sums(use_x, first, (own, coords[2]))
        part = late_sums(use_x, acc, (coords[1], coords[3]), then)
        sums.append([part[0]] + [cross(part[k], axis, k) for k in (1, 2, 3)])
    keep, give = combine(1 - jnp.bitwise_xor(c, yl), *sums)
    got = shift(give, "yl", 1)
    held = hold((projector, beside_w))
    return last_stage(at, keep, got, first_moment, second_moment, (*held, across_w), near_w)


def solution(mesh):
    fine = Mesh(mesh.devices.reshape(4, 4, 2, 2, 2), ("x", "z", "yl", "yh", "c"))
    dp, mp = ("x", "z", "yl"), ("yh", "c")
    return jax.shard_map(
        step,
        mesh=fine,
        in_specs=(P(dp, mp), P(dp, mp), P(dp, mp), P(mp, None), P(mp + dp, None), P(mp + dp, None)),
        out_specs=(P(mp + dp, None),) * 3,
        check_vma=False,
    )
```

```python
import jax
import jax.numpy as jnp
from jax import lax
from jax.experimental import pallas as pl
from jax.experimental.pallas import tpu as pltpu
from jax.sharding import Mesh, PartitionSpec as P


F32 = jnp.float32
BF16 = jnp.bfloat16
SIZE = {"x": 4, "z": 4, "yl": 2, "yh": 2, "c": 2}
SMEM = pl.BlockSpec(memory_space=pltpu.SMEM)
VMEM = pl.BlockSpec(memory_space=pltpu.VMEM)
HBM = pl.BlockSpec(memory_space=pl.ANY)
AXES = ("x", "z", "yl", "yh", "c")


def params(mib):
    return pltpu.CompilerParams(vmem_limit_bytes=mib * 1024 * 1024)


def shift(a, axis, k):
    n = SIZE[axis]
    return lax.ppermute(a, axis, [(i, (i + k) % n) for i in range(n)])


def cross(a, first, k):
    pairs = []
    for i in range(128):
        x, z, rest = i // 32, i // 8 % 4, i % 8
        if (i % 2 == 0) == (first == "x"):
            x = (x + k) % 4
        else:
            z = (z + k) % 4
        pairs.append((i, x * 32 + z * 8 + rest))
    return lax.ppermute(a, AXES, pairs)


def front_kernel(s_ref, g_ref, h_ref, i_ref, w_ref, mine, theirs, *rest):
    outs, t_ref = rest[:-1], rest[-1]
    to_x, to_z = outs[:4], outs[4:]
    i = pl.program_id(0)
    for b in range(14):
        cols = slice(b * 128, b * 128 + 128)
        v = 0.5 * g_ref[:, cols].astype(F32)
        w = v * h_ref[:, cols].astype(F32)
        t_ref[cols, :] = (w + w * jnp.tanh(v)).astype(BF16).T
    c = s_ref[2]
    for out, half in ((mine, c), (theirs, 1 - c)):
        start = pl.multiple_of(half * 256, 256)
        part = jnp.dot(i_ref[...], w_ref[:, pl.ds(start, 256)], preferred_element_type=F32)

        @pl.when(i == 0)
        def _():
            out[...] = part

        @pl.when(i > 0)
        def _():
            out[...] += part

    for k in range(4):
        start = pl.multiple_of(lax.rem(s_ref[1] + k, 4) * 448, 448)
        to_z[k][i] = t_ref[pl.ds(start + 224, 224), :]
        for j in range(4):

            @pl.when(i == j)
            def _():
                to_x[j][k] = t_ref[pl.ds(start, 224), :]


def front(at, gate, hidden, inputs, projector):
    t = gate.shape[0]
    block = pl.BlockSpec((t, 1792), lambda i, s: (0, lax.rem(s[0] + i, 4)))
    args = [
        pltpu.with_memory_space_constraint(a, pltpu.HBM) for a in (gate, hidden, inputs, projector)
    ]
    return pl.pallas_call(
        front_kernel,
        grid_spec=pltpu.PrefetchScalarGridSpec(
            num_scalar_prefetch=1,
            grid=(4,),
            in_specs=[
                block,
                block,
                pl.BlockSpec((t, 512), lambda i, s: (0, i)),
                pl.BlockSpec((512, 512), lambda i, s: (i, 0)),
            ],
            out_specs=[VMEM] * 10,
            scratch_shapes=[pltpu.VMEM((1792, t), BF16)],
        ),
        out_shape=[pltpu.VMEM((t, 256), F32)] * 2 + [pltpu.VMEM((4, 224, t), BF16)] * 8,
        compiler_params=params(16),
        name="front",
    )(at, *args)


def join_kernel(s_ref, half, other, out):
    c = s_ref[2]
    out[:, pl.ds(pl.multiple_of(c * 256, 256), 256)] = half[...]
    out[:, pl.ds(pl.multiple_of(256 - c * 256, 256), 256)] = other[...]


def join(at, half, other):
    args = [pltpu.with_memory_space_constraint(a, pltpu.VMEM) for a in (half, other)]
    return pl.pallas_call(
        join_kernel,
        in_specs=[SMEM, VMEM, VMEM],
        out_specs=VMEM,
        out_shape=pltpu.VMEM((half.shape[0], 512), BF16),
        compiler_params=params(4),
        name="join",
    )(at, *args)


def hold_kernel(a, b, x, y, sem):
    copies = []
    for k, (src, dst) in enumerate(((a, x), (b, y))):
        for q in range(2):
            rows = pl.ds(q * 1024, 1024)
            copies.append(pltpu.make_async_copy(src.at[rows], dst.at[rows], sem.at[2 * k + q]))
    for copy in copies:
        copy.start()
    for copy in copies:
        copy.wait()


def hold(blocks):
    args = [pltpu.with_memory_space_constraint(a, pltpu.HBM) for a in blocks]
    return pl.pallas_call(
        hold_kernel,
        in_specs=[HBM] * 2,
        out_specs=[VMEM] * 2,
        out_shape=[pltpu.VMEM((2048, 512), BF16)] * 2,
        scratch_shapes=[pltpu.SemaphoreType.DMA((4,))],
        compiler_params=params(1),
        name="keep",
    )(*args)


def load(use_x, piece_x, piece_z, dst, sem):
    for use, src in ((1, piece_x), (0, piece_z)):

        @pl.when(use_x == use)
        def _():
            pltpu.make_async_copy(src, dst, sem).start()

    return pltpu.make_async_copy(piece_x, dst, sem)


def early_kernel(s_ref, x0, x2, z0, z2, c0, c2, *rest):
    n_more = (len(rest) - 5) // 2
    more, (out, *kept), (lhs, rhs, sem, more_sem) = rest[:n_more], rest[n_more:-4], rest[-4:]
    copies = [pltpu.make_async_copy(a, b, more_sem.at[k]) for k, (a, b) in enumerate(zip(more, kept))]
    for copy in copies:
        copy.start()
    loads = [
        [
            load(s_ref[0], a.at[j], b.at[j], lhs.at[j, :, pl.ds(n * 384, 384)], sem.at[j, n])
            for n, (a, b) in enumerate(((x0, z0), (x2, z2)))
        ]
        for j in range(4)
    ]
    for n, coords in enumerate((c0, c2)):
        rhs[n * 384 : n * 384 + 384, :] = coords[...]
    for j in range(4):
        for copy in loads[j]:
            copy.wait()
        out[j] = jnp.dot(lhs[j], rhs[...], preferred_element_type=F32)
    for copy in copies:
        copy.wait()


def early_sums(use_x, pieces, coords, more):
    t = pieces[0].shape[-1]
    args = [pltpu.with_memory_space_constraint(a, pltpu.HBM) for a in pieces]
    args += [pltpu.with_memory_space_constraint(a, pltpu.VMEM) for a in coords]
    args += [pltpu.with_memory_space_constraint(a, pltpu.HBM) for a in more]
    return pl.pallas_call(
        early_kernel,
        in_specs=[SMEM] + [HBM] * 4 + [VMEM] * 2 + [HBM] * len(more),
        out_specs=[VMEM] * (1 + len(more)),
        out_shape=[pltpu.VMEM((4, 224, 512), F32)] + [pltpu.VMEM(a.shape, a.dtype) for a in more],
        scratch_shapes=[
            pltpu.VMEM((4, 224, 2 * t), BF16),
            pltpu.VMEM((2 * t, 512), BF16),
            pltpu.SemaphoreType.DMA((4, 2)),
            pltpu.SemaphoreType.DMA((2,)),
        ],
        compiler_params=params(8),
    )(use_x.reshape(1), *args)


def late_kernel(s_ref, acc_m, acc_t, c1m, c3m, c1t, c3t, x1, x3, z1, z3, *rest):
    outs_m, outs_t, (own, sem) = rest[:4], rest[4:8], rest[8:]
    sides = ((acc_m, c1m, c3m, outs_m), (acc_t, c1t, c3t, outs_t))
    writes = [pltpu.make_async_copy(own.at[n], side[3][0], sem.at[n]) for n, side in enumerate(sides)]
    for use, pieces in ((1, ((x1, x3), (z1, z3))), (0, ((z1, z3), (x1, x3)))):

        @pl.when(s_ref[0] == use)
        def _():
            for n, ((acc, c1, c3, outs), (ones, threes)) in enumerate(zip(sides, pieces)):
                for j, out in enumerate((own.at[n], *outs[1:])):
                    part = acc[j] + jnp.dot(ones[j], c1[...], preferred_element_type=F32)
                    part += jnp.dot(threes[j], c3[...], preferred_element_type=F32)
                    out[...] = part.astype(out.dtype)
                    if j == 0:
                        writes[n].start()

    for write in writes:
        write.wait()


def late_sums(mine_x, accs, coords, pieces):
    args = [pltpu.with_memory_space_constraint(a, pltpu.VMEM) for a in (*accs, *coords, *pieces)]
    out_specs = [pl.BlockSpec(memory_space=pltpu.HBM)] + [VMEM] * 3
    out_shape = [pltpu.HBM((224, 512), F32)] + [pltpu.VMEM((224, 512), BF16)] * 3
    return pl.pallas_call(
        late_kernel,
        in_specs=[SMEM] + [VMEM] * 10,
        out_specs=out_specs * 2,
        out_shape=out_shape * 2,
        scratch_shapes=[pltpu.VMEM((2, 224, 512), F32), pltpu.SemaphoreType.DMA((2,))],
        compiler_params=params(6),
        name="late",
    )(mine_x.reshape(1), *args)


def combine_kernel(s_ref, m0, m1, m2, m3, t0, t1, t2, t3, keep, give):
    mine = m0[...] + m1[...].astype(F32) + m2[...].astype(F32) + m3[...].astype(F32)
    theirs = t0[...] + t1[...].astype(F32) + t2[...].astype(F32) + t3[...].astype(F32)
    here = s_ref[0] == 1
    keep[...] = jnp.where(here, mine, theirs)
    give[...] = jnp.where(here, theirs, mine).astype(BF16)


def combine(keep_mine, mine, theirs):
    args = [pltpu.with_memory_space_constraint(a, pltpu.VMEM) for a in (*mine, *theirs)]
    return pl.pallas_call(
        combine_kernel,
        in_specs=[SMEM] + [VMEM] * 8,
        out_specs=[VMEM] * 2,
        out_shape=[pltpu.VMEM((224, 512), F32), pltpu.VMEM((224, 512), BF16)],
        compiler_params=params(4),
        name="combine",
    )(keep_mine.reshape(1), *args)


def last_kernel(
    s_ref, mine, got, first, second, w0, w1, w2, w3, new_first, new_second, update,
    w_ref, m_ref, o_ref, w_sem, m_sem, o_sem,
):
    yh, c = s_ref[3], s_ref[2]
    loads = []
    for q in range(2):
        rows = pl.ds(q * 1024, 1024)
        loads.append(pltpu.make_async_copy(w3.at[rows], w_ref.at[rows], w_sem.at[q]))
        loads[q].start()
    projected = mine[...] + got[...].astype(F32)
    m = 0.9 * first[...] + 0.1 * projected
    v = 0.95 * second[...] + 0.05 * projected * projected
    m_ref[0] = m
    m_ref[1] = v
    stores = [
        pltpu.make_async_copy(m_ref.at[k], out, m_sem.at[k])
        for k, out in enumerate((new_first, new_second))
    ]
    for out in stores:
        out.start()
    root = jnp.sqrt(v * (1.0 / (1.0 - 0.9025)))
    direction = (m * (1.0 / (1.0 - 0.81)) / (root + 1e-08)).astype(BF16)
    blocks = (2 * yh + c, 2 * yh + 1 - c, 3 - 2 * yh - c, 2 - 2 * yh + c)
    for k, w in enumerate((w0, w1, w2, w_ref)):
        for q in range(2):
            if k == 3:
                loads[q].wait()
            part = 4.0 * lax.dot_general(
                direction,
                w[q * 1024 : q * 1024 + 1024, :],
                (((1,), (1,)), ((), ())),
                preferred_element_type=F32,
            )
            o_ref[2 * k + q] = part.astype(BF16)
            cols = pl.ds(pl.multiple_of(blocks[k] * 2048 + q * 1024, 1024), 1024)
            out = pltpu.make_async_copy(o_ref.at[2 * k + q], update.at[:, cols], o_sem.at[2 * k + q])
            out.start()
            stores.append(out)
    for out in stores:
        out.wait()


def last_stage(at, mine, got, first, second, blocks, near):
    rows = first.shape[0]
    moment = jax.ShapeDtypeStruct((rows, 512), F32)
    args = [
        pltpu.with_memory_space_constraint(a, pltpu.VMEM)
        for a in (mine, got, first, second) + tuple(blocks)
    ]
    args.append(pltpu.with_memory_space_constraint(near, pltpu.HBM))
    return pl.pallas_call(
        last_kernel,
        in_specs=[SMEM] + [VMEM] * 7 + [HBM],
        out_specs=[HBM] * 3,
        out_shape=[moment, moment, jax.ShapeDtypeStruct((rows, 8192), BF16)],
        scratch_shapes=[
            pltpu.VMEM((2048, 512), BF16),
            pltpu.VMEM((2, rows, 512), F32),
            pltpu.VMEM((8, rows, 1024), BF16),
            pltpu.SemaphoreType.DMA((2,)),
            pltpu.SemaphoreType.DMA((2,)),
            pltpu.SemaphoreType.DMA((8,)),
        ],
        compiler_params=params(12),
        name="last",
    )(at, *args)


def step(inputs, gate_preact, hidden_grad, projector, first_moment, second_moment):
    x, z, yl, yh, c = (lax.axis_index(a).astype(jnp.int32) for a in AXES)
    at = jnp.stack([x, z, c, yh])

    mine, theirs, *pieces = front(at, gate_preact, hidden_grad, inputs, projector)
    got_x = [pieces[0]] + [shift(pieces[k], "x", k) for k in (1, 2, 3)]
    got_z = [pieces[4]] + [shift(pieces[4 + k], "z", k) for k in (1, 2, 3)]

    chip_sum = mine + shift(theirs, "c", 1)
    far = shift(chip_sum.astype(BF16), "yh", 1)
    half = (chip_sum + far.astype(F32)).astype(BF16)
    own = join(at, half, shift(half, "c", 1))
    along = {k: cross(own, "x", k) for k in (1, 3, 2)}
    beyond = {k: shift(along[k], "c", 1) for k in (1, 3, 2)}

    near_w = lax.ppermute(projector, ("yl", "yh"), [(0, 3), (3, 0), (1, 2), (2, 1)])
    beside_w = shift(projector, "c", 1)
    across_w = shift(near_w, "c", 1)

    first = [got[k] for got in (got_x, got_z) for k in (0, 2)]
    then = [got[k] for got in (got_x, got_z) for k in (1, 3)]
    acc_m = early_sums(1 - c, first, (own, along[2]), ())[0]
    acc_t, *moved = early_sums(c, first, (own, beyond[2]), (along[1], along[3]))
    part = late_sums(1 - c, (acc_m, acc_t), (*moved, beyond[1], beyond[3]), then)
    sums = [
        [own_part] + [cross(sent[k - 1], axis, k) for k in (1, 2, 3)]
        for own_part, sent, axis in ((part[0], part[1:4], "z"), (part[4], part[5:], "x"))
    ]
    keep, give = combine(1 - jnp.bitwise_xor(c, yl), *sums)
    got = shift(give, "yl", 1)
    held = hold((projector, beside_w))
    return last_stage(at, keep, got, first_moment, second_moment, (*held, across_w), near_w)


def solution(mesh):
    fine = Mesh(mesh.devices.reshape(4, 4, 2, 2, 2), ("x", "z", "yl", "yh", "c"))
    dp, mp = ("x", "z", "yl"), ("yh", "c")
    return jax.shard_map(
        step,
        mesh=fine,
        in_specs=(P(dp, mp), P(dp, mp), P(dp, mp), P(mp, None), P(mp + dp, None), P(mp + dp, None)),
        out_specs=(P(mp + dp, None),) * 3,
        check_vma=False,
    )
```

```python
import jax
import jax.numpy as jnp
from jax import lax
from jax.experimental import pallas as pl
from jax.experimental.pallas import tpu as pltpu
from jax.sharding import Mesh, PartitionSpec as P


F32 = jnp.float32
BF16 = jnp.bfloat16
SIZE = {"x": 4, "z": 4, "yl": 2, "yh": 2, "c": 2}
SMEM = pl.BlockSpec(memory_space=pltpu.SMEM)
VMEM = pl.BlockSpec(memory_space=pltpu.VMEM)
HBM = pl.BlockSpec(memory_space=pl.ANY)
AXES = ("x", "z", "yl", "yh", "c")


def params(mib):
    return pltpu.CompilerParams(vmem_limit_bytes=mib * 1024 * 1024)


def shift(a, axis, k):
    n = SIZE[axis]
    return lax.ppermute(a, axis, [(i, (i + k) % n) for i in range(n)])


def cross(a, first, k):
    pairs = []
    for i in range(128):
        x, z, rest = i // 32, i // 8 % 4, i % 8
        if (i % 2 == 0) == (first == "x"):
            x = (x + k) % 4
        else:
            z = (z + k) % 4
        pairs.append((i, x * 32 + z * 8 + rest))
    return lax.ppermute(a, AXES, pairs)


def front_kernel(s_ref, g_ref, h_ref, i_ref, w_ref, mine, theirs, *rest):
    outs, t_ref = rest[:-1], rest[-1]
    to_x, to_z = outs[:4], outs[4:]
    i = pl.program_id(0)
    for b in range(14):
        cols = slice(b * 128, b * 128 + 128)
        v = 0.5 * g_ref[:, cols].astype(F32)
        w = v * h_ref[:, cols].astype(F32)
        t_ref[cols, :] = (w + w * jnp.tanh(v)).astype(BF16).T
    c = s_ref[2]
    for out, half in ((mine, c), (theirs, 1 - c)):
        start = pl.multiple_of(half * 256, 256)
        part = jnp.dot(i_ref[...], w_ref[:, pl.ds(start, 256)], preferred_element_type=F32)

        @pl.when(i == 0)
        def _():
            out[...] = part

        @pl.when(i > 0)
        def _():
            out[...] += part

    for k in range(4):
        start = pl.multiple_of(lax.rem(s_ref[1] + k, 4) * 448, 448)
        to_z[k][i] = t_ref[pl.ds(start + 224, 224), :]
        for j in range(4):

            @pl.when(i == j)
            def _():
                to_x[j][k] = t_ref[pl.ds(start, 224), :]


def front(at, gate, hidden, inputs, projector):
    t = gate.shape[0]
    block = pl.BlockSpec((t, 1792), lambda i, s: (0, lax.rem(s[0] + i, 4)))
    args = [
        pltpu.with_memory_space_constraint(a, pltpu.HBM) for a in (gate, hidden, inputs, projector)
    ]
    return pl.pallas_call(
        front_kernel,
        grid_spec=pltpu.PrefetchScalarGridSpec(
            num_scalar_prefetch=1,
            grid=(4,),
            in_specs=[
                block,
                block,
                pl.BlockSpec((t, 512), lambda i, s: (0, i)),
                pl.BlockSpec((512, 512), lambda i, s: (i, 0)),
            ],
            out_specs=[VMEM] * 10,
            scratch_shapes=[pltpu.VMEM((1792, t), BF16)],
        ),
        out_shape=[pltpu.VMEM((t, 256), F32)] * 2 + [pltpu.VMEM((4, 224, t), BF16)] * 8,
        compiler_params=params(16),
        name="front",
    )(at, *args)


def join_kernel(s_ref, half, other, out):
    c = s_ref[2]
    out[:, pl.ds(pl.multiple_of(c * 256, 256), 256)] = half[...]
    out[:, pl.ds(pl.multiple_of(256 - c * 256, 256), 256)] = other[...]


def join(at, half, other):
    args = [pltpu.with_memory_space_constraint(a, pltpu.VMEM) for a in (half, other)]
    return pl.pallas_call(
        join_kernel,
        in_specs=[SMEM, VMEM, VMEM],
        out_specs=VMEM,
        out_shape=pltpu.VMEM((half.shape[0], 512), BF16),
        compiler_params=params(4),
        name="join",
    )(at, *args)


def hold_kernel(a, b, x, y, sem):
    copies = []
    for k, (src, dst) in enumerate(((a, x), (b, y))):
        for q in range(2):
            rows = pl.ds(q * 1024, 1024)
            copies.append(pltpu.make_async_copy(src.at[rows], dst.at[rows], sem.at[2 * k + q]))
    for copy in copies:
        copy.start()
    for copy in copies:
        copy.wait()


def hold(blocks):
    args = [pltpu.with_memory_space_constraint(a, pltpu.HBM) for a in blocks]
    return pl.pallas_call(
        hold_kernel,
        in_specs=[HBM] * 2,
        out_specs=[VMEM] * 2,
        out_shape=[pltpu.VMEM((2048, 512), BF16)] * 2,
        scratch_shapes=[pltpu.SemaphoreType.DMA((4,))],
        compiler_params=params(1),
        name="keep",
    )(*args)


def load(use_x, piece_x, piece_z, dst, sem):
    for use, src in ((1, piece_x), (0, piece_z)):

        @pl.when(use_x == use)
        def _():
            pltpu.make_async_copy(src, dst, sem).start()

    return pltpu.make_async_copy(piece_x, dst, sem)


def early_kernel(s_ref, x0, x2, z0, z2, c0, c2, *rest):
    n_more = (len(rest) - 5) // 2
    more, (out, *kept), (lhs, rhs, sem, more_sem) = rest[:n_more], rest[n_more:-4], rest[-4:]
    copies = [pltpu.make_async_copy(a, b, more_sem.at[k]) for k, (a, b) in enumerate(zip(more, kept))]
    for copy in copies:
        copy.start()
    loads = [
        [
            load(s_ref[0], a.at[j], b.at[j], lhs.at[j, :, pl.ds(n * 384, 384)], sem.at[j, n])
            for n, (a, b) in enumerate(((x0, z0), (x2, z2)))
        ]
        for j in range(4)
    ]
    for n, coords in enumerate((c0, c2)):
        rhs[n * 384 : n * 384 + 384, :] = coords[...]
    for j in range(4):
        for copy in loads[j]:
            copy.wait()
        out[j] = jnp.dot(lhs[j], rhs[...], preferred_element_type=F32)
    for copy in copies:
        copy.wait()


def early_sums(use_x, pieces, coords, more):
    t = pieces[0].shape[-1]
    args = [pltpu.with_memory_space_constraint(a, pltpu.HBM) for a in pieces]
    args += [pltpu.with_memory_space_constraint(a, pltpu.VMEM) for a in coords]
    args += [pltpu.with_memory_space_constraint(a, pltpu.HBM) for a in more]
    return pl.pallas_call(
        early_kernel,
        in_specs=[SMEM] + [HBM] * 4 + [VMEM] * 2 + [HBM] * len(more),
        out_specs=[VMEM] * (1 + len(more)),
        out_shape=[pltpu.VMEM((4, 224, 512), F32)] + [pltpu.VMEM(a.shape, a.dtype) for a in more],
        scratch_shapes=[
            pltpu.VMEM((4, 224, 2 * t), BF16),
            pltpu.VMEM((2 * t, 512), BF16),
            pltpu.SemaphoreType.DMA((4, 2)),
            pltpu.SemaphoreType.DMA((2,)),
        ],
        compiler_params=params(8),
    )(use_x.reshape(1), *args)


def late_kernel(s_ref, acc, c1, c3, x1, x3, z1, z3, o0, o1, o2, o3, own, sem):
    write = pltpu.make_async_copy(own, o0, sem)
    for use, ones, threes in ((1, x1, x3), (0, z1, z3)):

        @pl.when(s_ref[0] == use)
        def _():
            for j, out in enumerate((own, o1, o2, o3)):
                part = acc[j] + jnp.dot(ones[j], c1[...], preferred_element_type=F32)
                part += jnp.dot(threes[j], c3[...], preferred_element_type=F32)
                out[...] = part.astype(out.dtype)
                if j == 0:
                    write.start()

    write.wait()


def late_sums(use_x, acc, coords, pieces):
    args = [pltpu.with_memory_space_constraint(a, pltpu.VMEM) for a in (acc, *coords, *pieces)]
    return pl.pallas_call(
        late_kernel,
        in_specs=[SMEM] + [VMEM] * 7,
        out_specs=[pl.BlockSpec(memory_space=pltpu.HBM)] + [VMEM] * 3,
        out_shape=[pltpu.HBM((224, 512), F32)] + [pltpu.VMEM((224, 512), BF16)] * 3,
        scratch_shapes=[pltpu.VMEM((224, 512), F32), pltpu.SemaphoreType.DMA],
        compiler_params=params(6),
    )(use_x.reshape(1), *args)


def combine_kernel(s_ref, m0, m1, m2, m3, t0, t1, t2, t3, keep, give):
    mine = m0[...] + m1[...].astype(F32) + m2[...].astype(F32) + m3[...].astype(F32)
    theirs = t0[...] + t1[...].astype(F32) + t2[...].astype(F32) + t3[...].astype(F32)
    here = s_ref[0] == 1
    keep[...] = jnp.where(here, mine, theirs)
    give[...] = jnp.where(here, theirs, mine).astype(BF16)


def combine(keep_mine, mine, theirs):
    args = [pltpu.with_memory_space_constraint(a, pltpu.VMEM) for a in (*mine, *theirs)]
    return pl.pallas_call(
        combine_kernel,
        in_specs=[SMEM] + [VMEM] * 8,
        out_specs=[VMEM] * 2,
        out_shape=[pltpu.VMEM((224, 512), F32), pltpu.VMEM((224, 512), BF16)],
        compiler_params=params(4),
        name="combine",
    )(keep_mine.reshape(1), *args)


def last_kernel(
    s_ref, mine, got, first, second, w0, w1, w2, w3, new_first, new_second, update,
    w_ref, m_ref, o_ref, w_sem, m_sem, o_sem,
):
    yh, c = s_ref[3], s_ref[2]
    loads = []
    for q in range(2):
        rows = pl.ds(q * 1024, 1024)
        loads.append(pltpu.make_async_copy(w3.at[rows], w_ref.at[rows], w_sem.at[q]))
        loads[q].start()
    projected = mine[...] + got[...].astype(F32)
    m = 0.9 * first[...] + 0.1 * projected
    v = 0.95 * second[...] + 0.05 * projected * projected
    m_ref[0] = m
    m_ref[1] = v
    stores = [
        pltpu.make_async_copy(m_ref.at[k], out, m_sem.at[k])
        for k, out in enumerate((new_first, new_second))
    ]
    for out in stores:
        out.start()
    root = jnp.sqrt(v * (1.0 / (1.0 - 0.9025)))
    direction = (m * (1.0 / (1.0 - 0.81)) / (root + 1e-08)).astype(BF16)
    blocks = (2 * yh + c, 2 * yh + 1 - c, 3 - 2 * yh - c, 2 - 2 * yh + c)
    for k, w in enumerate((w0, w1, w2, w_ref)):
        for q in range(2):
            if k == 3:
                loads[q].wait()
            part = 4.0 * lax.dot_general(
                direction,
                w[q * 1024 : q * 1024 + 1024, :],
                (((1,), (1,)), ((), ())),
                preferred_element_type=F32,
            )
            o_ref[2 * k + q] = part.astype(BF16)
            cols = pl.ds(pl.multiple_of(blocks[k] * 2048 + q * 1024, 1024), 1024)
            out = pltpu.make_async_copy(o_ref.at[2 * k + q], update.at[:, cols], o_sem.at[2 * k + q])
            out.start()
            stores.append(out)
    for out in stores:
        out.wait()


def last_stage(at, mine, got, first, second, blocks, near):
    rows = first.shape[0]
    moment = jax.ShapeDtypeStruct((rows, 512), F32)
    args = [
        pltpu.with_memory_space_constraint(a, pltpu.VMEM)
        for a in (mine, got, first, second) + tuple(blocks)
    ]
    args.append(pltpu.with_memory_space_constraint(near, pltpu.HBM))
    return pl.pallas_call(
        last_kernel,
        in_specs=[SMEM] + [VMEM] * 7 + [HBM],
        out_specs=[HBM] * 3,
        out_shape=[moment, moment, jax.ShapeDtypeStruct((rows, 8192), BF16)],
        scratch_shapes=[
            pltpu.VMEM((2048, 512), BF16),
            pltpu.VMEM((2, rows, 512), F32),
            pltpu.VMEM((8, rows, 1024), BF16),
            pltpu.SemaphoreType.DMA((2,)),
            pltpu.SemaphoreType.DMA((2,)),
            pltpu.SemaphoreType.DMA((8,)),
        ],
        compiler_params=params(12),
        name="last",
    )(at, *args)


def step(inputs, gate_preact, hidden_grad, projector, first_moment, second_moment):
    x, z, yl, yh, c = (lax.axis_index(a).astype(jnp.int32) for a in AXES)
    at = jnp.stack([x, z, c, yh])

    mine, theirs, *pieces = front(at, gate_preact, hidden_grad, inputs, projector)
    got_x = [pieces[0]] + [shift(pieces[k], "x", k) for k in (1, 2, 3)]
    got_z = [pieces[4]] + [shift(pieces[4 + k], "z", k) for k in (1, 2, 3)]

    chip_sum = mine + shift(theirs, "c", 1)
    far = shift(chip_sum.astype(BF16), "yh", 1)
    half = (chip_sum + far.astype(F32)).astype(BF16)
    own = join(at, half, shift(half, "c", 1))
    along = {k: cross(own, "x", k) for k in (1, 3, 2)}
    beyond = {k: shift(along[k], "c", 1) for k in (1, 3, 2)}

    near_w = lax.ppermute(projector, ("yl", "yh"), [(0, 3), (3, 0), (1, 2), (2, 1)])
    beside_w = shift(projector, "c", 1)
    across_w = shift(near_w, "c", 1)

    first = [got[k] for got in (got_x, got_z) for k in (0, 2)]
    then = [got[k] for got in (got_x, got_z) for k in (1, 3)]
    acc_m = early_sums(1 - c, first, (own, along[2]), ())[0]
    acc_t, *moved = early_sums(c, first, (own, beyond[2]), (along[1], along[3]))
    sums = []
    for use_x, acc, coords, axis in (
        (1 - c, acc_m, moved, "z"), (c, acc_t, (beyond[1], beyond[3]), "x")
    ):
        part = late_sums(use_x, acc, coords, then)
        sums.append([part[0]] + [cross(part[k], axis, k) for k in (1, 2, 3)])
    keep, give = combine(1 - jnp.bitwise_xor(c, yl), *sums)
    got = shift(give, "yl", 1)
    held = hold((projector, beside_w))
    return last_stage(at, keep, got, first_moment, second_moment, (*held, across_w), near_w)


def solution(mesh):
    fine = Mesh(mesh.devices.reshape(4, 4, 2, 2, 2), ("x", "z", "yl", "yh", "c"))
    dp, mp = ("x", "z", "yl"), ("yh", "c")
    return jax.shard_map(
        step,
        mesh=fine,
        in_specs=(P(dp, mp), P(dp, mp), P(dp, mp), P(mp, None), P(mp + dp, None), P(mp + dp, None)),
        out_specs=(P(mp + dp, None),) * 3,
        check_vma=False,
    )
```
